512 devices in a mesh: tok: 16 (over y, core), voc: 32 (over x, z).
Axes of the slice: x: 4, y: 8, z: 8, core: 2. Of those that a mesh axis runs over, the one named last changes fastest.
Arguments:
- hidden: bfloat16 [4096, 2048], P('tok')
- panel: bfloat16 [2048, 8192], P(None, 'voc'), may hold values from -0.25 to 0.25
- in_proj: bfloat16 [2048, 64], replicated, may hold values from -0.125 to 0.125
- out_proj: bfloat16 [8192, 64], P('voc'), may hold values from -6 to 6
- targets: int32 [4096], P('tok'), may hold values from 0 to 8191
- keep: int32 [4096], P('tok'), may hold values 0 or 1
- span_ids: int32 [4096], P('tok'), may hold values from 0 to 511, as said below
- store: bfloat16 [131072, 4096], P(('tok', 'voc')), may hold values from -6 to 6
Outputs:
- hidden_grad: bfloat16 [4096, 2048], P('tok', 'voc')
- scores: float32 [512, 131072], P(None, ('tok', 'voc'))
The draws below stay inside these ranges and needn't reach their ends.
Inputs may be any that keep to these rules, and one draw needn't show every extreme that they name: `span_ids`: tokens k * 256 to (k + 1) * 256 - 1 hold exactly the spans k * 32 to (k + 1) * 32 - 1 in increasing order, each of one or more tokens.
All inputs are finite; a program needn't handle non-finite values. No bound on the sum of `keep` on one device may be relied on, other than what follows from the above.
Results may differ from the reference program's by a relative error of at most 0.018.
Values may be sent and summed in bfloat16 or wider, within the bound.
No kernel may reach another device: no remote copies, remote signals or barrier semaphores. Data moves between devices by JAX's collectives and lax.ppermute only.
A program may use at most 64 MiB of HBM per device.

```python
import math
import jax
import jax.numpy as jnp
import numpy as np
from jax import lax

D = 2048
PANEL = 8192
RANK = 64
TOK_DEV = 256
SPAN_DEV = 32
TOKENS = 4096
SPANS = 512
STORE_ROWS = 131072


def draw_hidden(key, part):
    values = jax.random.normal(jax.random.fold_in(key, 11), (TOKENS, D), jnp.float32)
    values = jnp.clip(values, -6.0, 6.0)
    return values.astype(jnp.bfloat16)


def draw_span_ids(key, part):
    blocks = TOKENS // TOK_DEV
    raw = jax.random.randint(jax.random.fold_in(key, 21), (blocks, TOK_DEV - 1), 0, 1 << 20)
    order = jnp.arange(TOK_DEV - 1, dtype=jnp.int32)
    ranked = jnp.argsort(raw * TOK_DEV + order[None, :], axis=1)
    cuts = ranked[:, :SPAN_DEV - 1].astype(jnp.int32) + 1
    position = jnp.arange(TOK_DEV, dtype=jnp.int32)
    local = jnp.sum((position[None, :, None] >= cuts[:, None, :]).astype(jnp.int32), axis=2)
    start = jnp.arange(blocks, dtype=jnp.int32)[:, None] * SPAN_DEV
    return (local + start).reshape(-1).astype(jnp.int32)


def plant(entries, key, least, high):
    longest = entries.shape.index(max(entries.shape))
    spots = []
    for shift in (0, 1):
        where = [jax.random.randint(jax.random.fold_in(key, axis), (), 0, length) for axis, length in enumerate(entries.shape)]
        where[longest] = (where[longest] + shift) % entries.shape[longest]
        spots.append(tuple(where))
    return entries.at[spots[0]].set(least).at[spots[1]].set(high)


def with_spikes(entries, key, source, target, shards_of, factor):
    def block_of(axis_at):
        return (jnp.arange(entries.shape[axis_at]) // (entries.shape[axis_at] // shards_of)).reshape((-1,) + (1,) * (entries.ndim - 1 - axis_at))

    one_side = jax.random.permutation(key, shards_of)[block_of(target)]
    far = (block_of(target) + shards_of // 2) % shards_of
    return jnp.where((block_of(source) == one_side) | (block_of(source) == far), factor * entries, entries)


def steps_of(key, extent, pieces, least, high):
    loudness, own = 1.0, jax.random.fold_in(key, 6)
    for dim, shards_of in pieces:
        steps = jnp.exp(jax.random.uniform(jax.random.fold_in(own, dim), (shards_of,), jnp.float32, least / len(pieces), high / len(pieces)))
        loudness = loudness * jnp.repeat(steps, extent[dim] // shards_of).reshape([-1 if axis == dim else 1 for axis in range(len(extent))])
    return loudness


def cumulative_ranks(number_of, lean):
    weights = [(1 << 20) // math.isqrt(grade ** lean) + 1 for grade in range(1, number_of + 1)]
    deviation = 1 + sum(weights) // (1 << 30)
    return np.cumsum(np.array([max(1, weight // deviation) for weight in weights]))


def skewed_ids(rng, shape, count, lean):
    table = cumulative_ranks(count, lean)
    pick = jax.random.randint(jax.random.fold_in(rng, 1), shape, 0, int(table[count - 1]))
    grade = jnp.searchsorted(jnp.asarray(table, jnp.int32), pick, side="right")
    return jax.random.permutation(jax.random.fold_in(rng, 2), count)[grade].astype(jnp.int32)


def scatter_about(stream_key, extent, spread, reach, pieces=(), held_as=jnp.bfloat16):
    entries = jax.random.normal(stream_key, extent, jnp.float32) * spread
    if len(pieces) > 0:
        entries = steps_of(stream_key, extent, pieces, -0.22, 0.18) * entries
    return jnp.clip(entries, min=-reach, max=reach).astype(held_as)


def heavy_noise(stream_key, extent, scale, bound, split, heavy, kind=jnp.bfloat16):
    result = scale * jax.random.normal(stream_key, extent, jnp.float32)
    if split:
        result = result * steps_of(stream_key, extent, split, -0.22, 0.18)
    return jnp.clip(with_spikes(result, jax.random.fold_in(stream_key, 3), *heavy), -bound, bound).astype(kind)


def setup_inputs(seed: int = 0) -> dict:
    key_of = jax.random.split(jax.random.key(seed), 9)
    return {
        "hidden": draw_hidden(jax.random.fold_in(key_of[8], 71), 0),
        "panel": heavy_noise(key_of[1], (D, PANEL), D ** -0.5, 0.25, ((1, 32),), (1, 0, 32, 2.75)),
        "in_proj": scatter_about(key_of[2], (D, RANK), D ** -0.5, 0.125),
        "out_proj": scatter_about(key_of[3], (PANEL, RANK), 1.0, 6.0, ((0, 32),)),
        "targets": plant(skewed_ids(key_of[4], (TOKENS,), PANEL, 2), jax.random.fold_in(key_of[4], 3), 0, PANEL - 1).astype(jnp.int32),
        "keep": plant((jax.random.randint(key_of[5], (TOKENS,), 0, 4) < 3).astype(jnp.int32), jax.random.fold_in(key_of[5], 1), 0, 1),
        "span_ids": draw_span_ids(jax.random.fold_in(key_of[8], 71), 0),
        "store": scatter_about(key_of[7], (STORE_ROWS, RANK * RANK), 1.0, 6.0, ((0, 512),)),
    }


def reference(hidden, panel, in_proj, out_proj, targets, keep, span_ids, store):
    logits = jnp.dot(hidden, panel, preferred_element_type=jnp.float32)
    top = jnp.max(logits, axis=1)
    total = jnp.sum(jnp.exp(logits - top[:, None]), axis=1)
    lse = top + jnp.log(total)
    columns = jnp.arange(PANEL, dtype=jnp.int32)
    onehot = (targets[:, None] == columns[None, :]).astype(jnp.float32)
    grad = ((jnp.exp(logits - lse[:, None]) - onehot) * keep.astype(jnp.float32)[:, None]).astype(jnp.bfloat16)
    hidden_grad = lax.dot_general(grad, panel, (((1,), (1,)), ((), ())), preferred_element_type=jnp.float32).astype(jnp.bfloat16)
    inner = jnp.dot(hidden, in_proj, preferred_element_type=jnp.float32)
    outer = jnp.dot(grad, out_proj, preferred_element_type=jnp.float32)
    product = (inner[:, :, None] * outer[:, None, :]).reshape(inner.shape[0], RANK * RANK)
    queries = jax.ops.segment_sum(product, span_ids, num_segments=SPANS).astype(jnp.bfloat16)
    scores = lax.dot_general(queries, store, (((1,), (1,)), ((), ())), preferred_element_type=jnp.float32) / RANK
    return hidden_grad, scores
```

```python
import functools

import jax
import jax.numpy as jnp
from jax import lax
from jax.experimental import pallas as pl
from jax.experimental.pallas import tpu as pltpu
from jax.sharding import PartitionSpec as P

RANK = 64
SPAN_DEV = 32
LOW = -1e30
F32 = jnp.float32
BF16 = jnp.bfloat16
LANES_BOTH = (((1,), (1,)), ((), ()))


def call(kernel, out_shape, **kw):
    return pl.pallas_call(kernel, out_shape=out_shape, **kw)


def vmem(n):
    return [pl.BlockSpec(memory_space=pltpu.VMEM)] * n


def logits_kernel(steps, base_ref, hid_ref, pan_ref, inp_ref, outp_ref, tgt_ref, span_ref,
                  logit_ref, msg_ref, inner_ref, acc, acc_in, rows):
    step = pl.program_id(0)
    part = jnp.dot(hid_ref[...], pan_ref[...], preferred_element_type=F32)
    part_in = lax.dot_general(inp_ref[...], hid_ref[...], LANES_BOTH, preferred_element_type=F32)

    @pl.when(step == 0)
    def _():
        acc[...] = part
        acc_in[...] = part_in

    @pl.when(step > 0)
    def _():
        acc[...] += part
        acc_in[...] += part_in

    @pl.when(step == steps - 1)
    def _():
        tokens = acc.shape[0]
        inner_ref[0:RANK, :] = acc_in[...].astype(BF16)
        inner_ref[RANK:, :] = jnp.broadcast_to(span_ref[...], (16, tokens)).astype(F32).astype(BF16)
        logit = acc[...].T
        logit_ref[...] = logit
        cols = lax.broadcasted_iota(jnp.int32, logit.shape, 0)
        hot = cols == tgt_ref[...] - base_ref[0]
        others = jnp.where(hot, LOW, logit)
        top = jnp.max(others, axis=0, keepdims=True)
        weight = jnp.exp(others - top)
        total = jnp.sum(weight, axis=0, keepdims=True)
        own = jnp.max(jnp.where(hot, logit, LOW), axis=0, keepdims=True)
        proj = outp_ref[...]
        rows[0:RANK, :] = jnp.dot(proj, weight.astype(BF16), preferred_element_type=F32)
        rows[RANK:, :] = jnp.dot(proj, hot.astype(F32).astype(BF16), preferred_element_type=F32)
        stats = jnp.concatenate([top, total, own], axis=0)
        devices = msg_ref.shape[0]
        share = RANK // devices
        for w in range(devices):
            msg_ref[w, 0:3, :] = stats
            msg_ref[w, 3 : 3 + share, :] = rows[share * w : share * (w + 1), :]
            msg_ref[w, 3 + share : 3 + 2 * share, :] = rows[RANK + share * w : RANK + share * (w + 1), :]
            msg_ref[w, 3 + 2 * share :, :] = jnp.zeros((5 - 2 * share, tokens), F32)


def combine_kernel(got_ref, keep_ref, out_ref, lse_ref, coef):
    devices = got_ref.shape[0]
    tops = got_ref[:, 0, :]
    totals = got_ref[:, 1, :]
    own = jnp.max(got_ref[:, 2, :], axis=0, keepdims=True)
    top = jnp.maximum(jnp.max(tops, axis=0, keepdims=True), own)
    scale = jnp.exp(tops - top)
    rest = jnp.sum(scale * totals, axis=0, keepdims=True)
    total = rest + jnp.exp(own - top)
    lse_ref[...] = top + jnp.log(total)
    keep = keep_ref[...].astype(F32)
    coef[...] = scale * (keep / total)
    gone = keep * (rest / total)
    part = jnp.zeros((2, top.shape[1]), F32)
    hot = jnp.zeros((2, top.shape[1]), F32)
    for v in range(devices):
        part += coef[v : v + 1, :] * got_ref[v, 3:5, :]
        hot += got_ref[v, 5:7, :]
    outer = (part - gone * hot).astype(BF16)
    out_ref[...] = jnp.broadcast_to(outer[None], out_ref.shape)


def scores_kernel(outer_ref, inner_ref, store_ref, out_ref, lhs, sums, query):
    groups = outer_ref.shape[0]
    tokens = outer_ref.shape[2]

    def group(k, carry):
        span = inner_ref[k, RANK : RANK + 1, :].astype(F32)
        block = jnp.floor(span * 0.125)
        row = span - 8.0 * block
        eight = (row == lax.broadcasted_iota(jnp.int32, (8, tokens), 0).astype(F32)).astype(F32)
        inner = inner_ref[k, 0:RANK, :].astype(F32)
        lhs[...] = (inner[:, None, :] * eight[None]).reshape(RANK * 8, tokens).astype(BF16)
        outer = outer_ref[k].astype(F32)
        right = jnp.concatenate(
            [outer * (block == float(j)).astype(F32) for j in range(4)], axis=0
        ).astype(BF16)
        sums[...] = lax.dot_general(lhs[...], right, LANES_BOTH, preferred_element_type=F32)
        for quad in range(RANK // 4):
            rows = [sums[pl.ds((4 * quad + i) * 8, 8), :] for i in range(4)]
            for j in range(0, 4, 2):
                both = [
                    jnp.concatenate([x[:, RANK * jj : RANK * (jj + 1)] for x in rows], axis=1)
                    for jj in (j, j + 1)
                ]
                query[pl.ds(pl.multiple_of(k * SPAN_DEV + 8 * j, 16), 16), 256 * quad : 256 * (quad + 1)] = (
                    jnp.concatenate(both, axis=0).astype(BF16)
                )
        return carry

    lax.fori_loop(0, groups, group, 0)
    out_ref[...] = lax.dot_general(
        query[...], store_ref[...], LANES_BOTH, preferred_element_type=F32
    ) * (1.0 / RANK)


def body(hidden, panel, in_proj, out_proj, targets, keep, span_ids, store):
    tokens, width = hidden.shape
    cols = panel.shape[1]
    devices = lax.axis_size("voc")
    share = width // devices
    base = lax.axis_index("voc") * cols
    local_span = span_ids - lax.axis_index("tok") * SPAN_DEV
    steps = 4
    piece = width // steps
    one = lambda i, b: (0, 0)
    logit, msg, inner = call(
        functools.partial(logits_kernel, steps),
        (
            jax.ShapeDtypeStruct((cols, tokens), F32),
            jax.ShapeDtypeStruct((devices, 8, tokens), F32),
            jax.ShapeDtypeStruct((RANK + 16, tokens), BF16),
        ),
        grid_spec=pltpu.PrefetchScalarGridSpec(
            num_scalar_prefetch=1,
            grid=(steps,),
            in_specs=[
                pl.BlockSpec((tokens, piece), lambda i, b: (0, i)),
                pl.BlockSpec((piece, cols), lambda i, b: (i, 0)),
                pl.BlockSpec((RANK, piece), lambda i, b: (0, i)),
                pl.BlockSpec((RANK, cols), one),
                pl.BlockSpec((1, tokens), one),
                pl.BlockSpec((1, tokens), one),
            ],
            out_specs=[
                pl.BlockSpec((cols, tokens), one),
                pl.BlockSpec((devices, 8, tokens), lambda i, b: (0, 0, 0)),
                pl.BlockSpec((RANK + 16, tokens), one),
            ],
            scratch_shapes=[
                pltpu.VMEM((tokens, cols), F32),
                pltpu.VMEM((RANK, tokens), F32),
                pltpu.VMEM((2 * RANK, tokens), F32),
            ],
        ),
        name="logits",
    )(base[None], hidden, panel, in_proj.T, out_proj.T, targets[None], local_span[None])
    with jax.named_scope("stats_move"):
        got = lax.all_to_all(msg, "voc", 0, 0, tiled=True)
    with jax.named_scope("inner_move"):
        all_inner = lax.all_gather(inner, "tok", axis=0)
    got, all_inner = lax.optimization_barrier((got, all_inner))
    outer, lse = call(
        combine_kernel,
        (
            jax.ShapeDtypeStruct((devices, 2, tokens), BF16),
            jax.ShapeDtypeStruct((1, tokens), F32),
        ),
        in_specs=vmem(2),
        out_specs=tuple(vmem(2)),
        scratch_shapes=[pltpu.VMEM((devices, tokens), F32)],
        name="combine",
    )(got, keep[None])
    with jax.named_scope("outer_move"):
        outer = lax.all_to_all(outer, "voc", 0, 0, tiled=True)
    with jax.named_scope("grad"):
        ids = base + lax.broadcasted_iota(jnp.int32, (cols, tokens), 0)
        onehot = (ids == targets[None]).astype(F32)
        grad = ((jnp.exp(logit - lse) - onehot) * keep.astype(F32)[None]).astype(BF16)
        partial = jnp.dot(panel, grad, preferred_element_type=F32).astype(BF16)
    partial = partial.reshape(devices, share, tokens)
    outer, partial = lax.optimization_barrier((outer, partial))
    with jax.named_scope("hidden_move"):
        parts = lax.all_to_all(partial, "voc", 0, 0, tiled=True)
    with jax.named_scope("gather_move"):
        all_outer = lax.all_gather(outer.reshape(RANK, tokens), "tok", axis=0)
    groups = all_outer.shape[0]
    scores = call(
        scores_kernel,
        jax.ShapeDtypeStruct((groups * SPAN_DEV, store.shape[0]), F32),
        in_specs=vmem(3),
        out_specs=vmem(1)[0],
        scratch_shapes=[
            pltpu.VMEM((RANK * 8, tokens), BF16),
            pltpu.VMEM((RANK * 8, RANK * 4), F32),
            pltpu.VMEM((groups * SPAN_DEV, RANK * RANK), BF16),
        ],
        name="scores",
    )(all_outer, all_inner, store)
    hidden_grad = jnp.sum(parts.astype(F32), axis=0).astype(BF16).T
    return (hidden_grad, scores)


def solution(mesh):
    placed = (
        P("tok", None),
        P(None, "voc"),
        P(),
        P("voc", None),
        P("tok"),
        P("tok"),
        P("tok"),
        P(("tok", "voc"), None),
    )
    return jax.shard_map(
        body,
        mesh=mesh,
        in_specs=placed,
        out_specs=(P("tok", "voc"), P(None, ("tok", "voc"))),
        check_vma=False,
    )
```

```python
import functools

import jax
import jax.numpy as jnp
from jax import lax
from jax.experimental import pallas as pl
from jax.experimental.pallas import tpu as pltpu
from jax.sharding import PartitionSpec as P


RANK = 64
SPAN_DEV = 32
LOW = -1e30
F32 = jnp.float32
BF16 = jnp.bfloat16
LANES_BOTH = (((1,), (1,)), ((), ()))


def call(kernel, out_shape, **kw):
    return pl.pallas_call(kernel, out_shape=out_shape, **kw)


def vmem(n):
    return [pl.BlockSpec(memory_space=pltpu.VMEM)] * n


def logits_kernel(steps, place_ref, hid_ref, pan_ref, inp_ref, outp_ref, tgt_ref, span_ref,
                  logit_ref, msg_ref, inner_ref, acc, acc_in, rows):
    step = pl.program_id(0)
    part = jnp.dot(hid_ref[...], pan_ref[...], preferred_element_type=F32)
    part_in = lax.dot_general(inp_ref[...], hid_ref[...], LANES_BOTH, preferred_element_type=F32)

    @pl.when(step == 0)
    def _():
        acc[...] = part
        acc_in[...] = part_in

    @pl.when(step > 0)
    def _():
        acc[...] += part
        acc_in[...] += part_in

    @pl.when(step == steps - 1)
    def _():
        tokens = acc.shape[0]
        inner_ref[0:RANK, :] = acc_in[...].astype(BF16)
        span = span_ref[...] - place_ref[1] * SPAN_DEV
        inner_ref[RANK:, :] = jnp.broadcast_to(span, (16, tokens)).astype(F32).astype(BF16)
        logit = acc[...].T
        logit_ref[...] = logit
        cols = lax.broadcasted_iota(jnp.int32, logit.shape, 0)
        hot = cols == tgt_ref[...] - place_ref[0]
        others = jnp.where(hot, LOW, logit)
        top = jnp.max(others, axis=0, keepdims=True)
        weight = jnp.exp(others - top)
        total = jnp.sum(weight, axis=0, keepdims=True)
        own = jnp.max(jnp.where(hot, logit, LOW), axis=0, keepdims=True)
        proj = outp_ref[...]
        rows[0:RANK, :] = jnp.dot(proj, weight.astype(BF16), preferred_element_type=F32)
        rows[RANK:, :] = jnp.dot(proj, hot.astype(F32).astype(BF16), preferred_element_type=F32)
        stats = jnp.concatenate([top, total, own], axis=0)
        devices = msg_ref.shape[0]
        share = RANK // devices
        for w in range(devices):
            msg_ref[w, 0:3, :] = stats
            msg_ref[w, 3 : 3 + share, :] = rows[share * w : share * (w + 1), :]
            msg_ref[w, 3 + share : 3 + 2 * share, :] = rows[RANK + share * w : RANK + share * (w + 1), :]
            msg_ref[w, 3 + 2 * share :, :] = jnp.zeros((5 - 2 * share, tokens), F32)


def combine_kernel(got_ref, keep_ref, out_ref, lse_ref, coef):
    devices = got_ref.shape[0]
    tops = got_ref[:, 0, :]
    totals = got_ref[:, 1, :]
    own = jnp.max(got_ref[:, 2, :], axis=0, keepdims=True)
    top = jnp.maximum(jnp.max(tops, axis=0, keepdims=True), own)
    scale = jnp.exp(tops - top)
    rest = jnp.sum(scale * totals, axis=0, keepdims=True)
    total = rest + jnp.exp(own - top)
    lse_ref[...] = top + jnp.log(total)
    keep = keep_ref[...].astype(F32)
    coef[...] = scale * (keep / total)
    gone = keep * (rest / total)
    part = jnp.zeros((2, top.shape[1]), F32)
    hot = jnp.zeros((2, top.shape[1]), F32)
    for v in range(devices):
        part += coef[v : v + 1, :] * got_ref[v, 3:5, :]
        hot += got_ref[v, 5:7, :]
    outer = (part - gone * hot).astype(BF16)
    out_ref[...] = jnp.broadcast_to(outer[None], out_ref.shape)


def scores_kernel(place_ref, outer_ref, inner_ref, store_ref, out_ref, lhs, sums, query):
    groups = outer_ref.shape[0]
    tokens = outer_ref.shape[2]

    def group(k, carry):
        far = place_ref[1] ^ k
        slot = ((far & 1) << 3) | ((far & 2) << 1) | ((far & 4) >> 1) | ((far & 8) >> 3)
        span = inner_ref[slot, RANK : RANK + 1, :].astype(F32)
        block = jnp.floor(span * 0.125)
        row = span - 8.0 * block
        eight = (row == lax.broadcasted_iota(jnp.int32, (8, tokens), 0).astype(F32)).astype(F32)
        inner = inner_ref[slot, 0:RANK, :].astype(F32)
        lhs[...] = (inner[:, None, :] * eight[None]).reshape(RANK * 8, tokens).astype(BF16)
        outer = outer_ref[k].astype(F32)
        right = jnp.concatenate(
            [outer * (block == float(j)).astype(F32) for j in range(4)], axis=0
        ).astype(BF16)
        sums[...] = lax.dot_general(lhs[...], right, LANES_BOTH, preferred_element_type=F32)
        for quad in range(RANK // 4):
            rows = [sums[pl.ds((4 * quad + i) * 8, 8), :] for i in range(4)]
            for j in range(0, 4, 2):
                both = [
                    jnp.concatenate([x[:, RANK * jj : RANK * (jj + 1)] for x in rows], axis=1)
                    for jj in (j, j + 1)
                ]
                query[pl.ds(pl.multiple_of(k * SPAN_DEV + 8 * j, 16), 16), 256 * quad : 256 * (quad + 1)] = (
                    jnp.concatenate(both, axis=0).astype(BF16)
                )
        return carry

    lax.fori_loop(0, groups, group, 0)
    out_ref[...] = lax.dot_general(
        query[...], store_ref[...], LANES_BOTH, preferred_element_type=F32
    ) * (1.0 / RANK)


def doubled(array, bit):
    there = lax.ppermute(array, "tok", [(k, k ^ bit) for k in range(lax.axis_size("tok"))])
    return jnp.concatenate([array, there], axis=0)


def body(hidden, panel, in_proj, out_proj, targets, keep, span_ids, store):
    tokens, width = hidden.shape
    cols = panel.shape[1]
    devices = lax.axis_size("voc")
    share = width // devices
    base = lax.axis_index("voc") * cols
    me = lax.axis_index("tok")
    place = jnp.stack([base, me])
    steps = 4
    piece = width // steps
    one = lambda i, b: (0, 0)
    logit, msg, inner = call(
        functools.partial(logits_kernel, steps),
        (
            jax.ShapeDtypeStruct((cols, tokens), F32),
            jax.ShapeDtypeStruct((devices, 8, tokens), F32),
            jax.ShapeDtypeStruct((RANK + 16, tokens), BF16),
        ),
        grid_spec=pltpu.PrefetchScalarGridSpec(
            num_scalar_prefetch=1,
            grid=(steps,),
            in_specs=[
                pl.BlockSpec((tokens, piece), lambda i, b: (0, i)),
                pl.BlockSpec((piece, cols), lambda i, b: (i, 0)),
                pl.BlockSpec((RANK, piece), lambda i, b: (0, i)),
                pl.BlockSpec((RANK, cols), one),
                pl.BlockSpec((1, tokens), one),
                pl.BlockSpec((1, tokens), one),
            ],
            out_specs=[
                pl.BlockSpec((cols, tokens), one),
                pl.BlockSpec((devices, 8, tokens), lambda i, b: (0, 0, 0)),
                pl.BlockSpec((RANK + 16, tokens), one),
            ],
            scratch_shapes=[
                pltpu.VMEM((tokens, cols), F32),
                pltpu.VMEM((RANK, tokens), F32),
                pltpu.VMEM((2 * RANK, tokens), F32),
            ],
        ),
        name="logits",
    )(place, hidden, panel, in_proj.T, out_proj.T, targets[None], span_ids[None])
    got = lax.all_to_all(msg, "voc", 0, 0, tiled=True)
    all_inner = doubled(doubled(inner[None], 8), 4)
    got, all_inner = lax.optimization_barrier((got, all_inner))
    outer, lse = call(
        combine_kernel,
        (
            jax.ShapeDtypeStruct((devices, 2, tokens), BF16),
            jax.ShapeDtypeStruct((1, tokens), F32),
        ),
        in_specs=vmem(2),
        out_specs=tuple(vmem(2)),
        scratch_shapes=[pltpu.VMEM((devices, tokens), F32)],
        name="combine",
    )(got, keep[None])
    outer, lse, all_inner = lax.optimization_barrier((outer, lse, all_inner))
    outer = lax.all_to_all(outer, "voc", 0, 0, tiled=True)
    ids = base + lax.broadcasted_iota(jnp.int32, (cols, tokens), 0)
    onehot = (ids == targets[None]).astype(F32)
    grad = ((jnp.exp(logit - lse) - onehot) * keep.astype(F32)[None]).astype(BF16)
    partial = jnp.dot(panel, grad, preferred_element_type=F32).astype(BF16)
    partial = partial.reshape(devices, share, tokens)
    all_inner = doubled(doubled(all_inner, 2), 1)
    outer, partial, all_inner = lax.optimization_barrier((outer, partial, all_inner))
    parts = lax.all_to_all(partial, "voc", 0, 0, tiled=True)
    all_outer = lax.all_gather(outer.reshape(RANK, tokens), "tok", axis=0)
    groups = all_outer.shape[0]
    scores = call(
        scores_kernel,
        jax.ShapeDtypeStruct((groups * SPAN_DEV, store.shape[0]), F32),
        in_specs=[pl.BlockSpec(memory_space=pltpu.SMEM)] + vmem(3),
        out_specs=vmem(1)[0],
        scratch_shapes=[
            pltpu.VMEM((RANK * 8, tokens), BF16),
            pltpu.VMEM((RANK * 8, RANK * 4), F32),
            pltpu.VMEM((groups * SPAN_DEV, RANK * RANK), BF16),
        ],
        name="scores",
    )(place, all_outer, all_inner, store)
    hidden_grad = jnp.sum(parts.astype(F32), axis=0).astype(BF16).T
    return (hidden_grad, scores)


def solution(mesh):
    placed = (
        P("tok", None),
        P(None, "voc"),
        P(),
        P("voc", None),
        P("tok"),
        P("tok"),
        P("tok"),
        P(("tok", "voc"), None),
    )

    return jax.shard_map(
        body,
        mesh=mesh,
        in_specs=placed,
        out_specs=(P("tok", "voc"), P(None, ("tok", "voc"))),
        check_vma=False,
    )
```

```python
import functools

import jax
import jax.numpy as jnp
from jax import lax
from jax.experimental import pallas as pl
from jax.experimental.pallas import tpu as pltpu
from jax.sharding import PartitionSpec as P

RANK = 64
SPAN_DEV = 32
LOW = -1e30
F32 = jnp.float32
BF16 = jnp.bfloat16
LANES_BOTH = (((1,), (1,)), ((), ()))


def resident(array):
    return pltpu.with_memory_space_constraint(array, pltpu.VMEM)


def call(kernel, out_shape, **kw):
    room = pltpu.CompilerParams(vmem_limit_bytes=16 << 20)
    return pl.pallas_call(kernel, out_shape=out_shape, compiler_params=room, **kw)


def vmem(n):
    return [pl.BlockSpec(memory_space=pltpu.VMEM)] * n


def logits_kernel(steps, hid_ref, pan_ref, inp_ref, outp_ref, tgt_ref, span_ref,
                  logit_ref, msg_ref, inner_ref, acc, acc_in, rows):
    step = pl.program_id(0)
    part = jnp.dot(hid_ref[...], pan_ref[...], preferred_element_type=F32)
    part_in = lax.dot_general(inp_ref[...], hid_ref[...], LANES_BOTH, preferred_element_type=F32)

    @pl.when(step == 0)
    def _():
        acc[...] = part
        acc_in[...] = part_in

    @pl.when(step > 0)
    def _():
        acc[...] += part
        acc_in[...] += part_in

    @pl.when(step == steps - 1)
    def _():
        tokens = acc.shape[0]
        inner_ref[0:RANK, :] = acc_in[...].astype(BF16)
        span = (span_ref[...] - lax.axis_index("tok") * SPAN_DEV).astype(F32)
        inner_ref[RANK:, :] = jnp.broadcast_to(span, (16, tokens)).astype(BF16)
        logit = acc[...].T
        logit_ref[...] = logit
        cols = lax.broadcasted_iota(jnp.int32, logit.shape, 0)
        hot = cols == tgt_ref[...] - lax.axis_index("voc") * acc.shape[1]
        others = jnp.where(hot, LOW, logit)
        top = jnp.max(others, axis=0, keepdims=True)
        weight = jnp.exp(others - top)
        total = jnp.sum(weight, axis=0, keepdims=True)
        own = jnp.max(jnp.where(hot, logit, LOW), axis=0, keepdims=True)
        proj = outp_ref[...]
        rows[0:RANK, :] = jnp.dot(proj, weight.astype(BF16), preferred_element_type=F32)
        rows[RANK:, :] = jnp.dot(proj, hot.astype(F32).astype(BF16), preferred_element_type=F32)
        stats = jnp.concatenate([top, total, own], axis=0)
        devices = msg_ref.shape[0]
        share = RANK // devices
        for w in range(devices):
            msg_ref[w, 0:3, :] = stats
            msg_ref[w, 3 : 3 + share, :] = rows[share * w : share * (w + 1), :]
            msg_ref[w, 3 + share : 3 + 2 * share, :] = rows[RANK + share * w : RANK + share * (w + 1), :]
            msg_ref[w, 3 + 2 * share :, :] = jnp.zeros((5 - 2 * share, tokens), F32)


def combine_kernel(got_ref, keep_ref, out_ref, lse_ref, coef):
    devices = got_ref.shape[0]
    tops = got_ref[:, 0, :]
    totals = got_ref[:, 1, :]
    own = jnp.max(got_ref[:, 2, :], axis=0, keepdims=True)
    top = jnp.maximum(jnp.max(tops, axis=0, keepdims=True), own)
    scale = jnp.exp(tops - top)
    rest = jnp.sum(scale * totals, axis=0, keepdims=True)
    total = rest + jnp.exp(own - top)
    lse_ref[...] = top + jnp.log(total)
    keep = keep_ref[...].astype(F32)
    coef[...] = scale * (keep / total)
    gone = keep * (rest / total)
    part = jnp.zeros((2, top.shape[1]), F32)
    hot = jnp.zeros((2, top.shape[1]), F32)
    for v in range(devices):
        part += coef[v : v + 1, :] * got_ref[v, 3:5, :]
        hot += got_ref[v, 5:7, :]
    outer = (part - gone * hot).astype(BF16)
    out_ref[...] = jnp.broadcast_to(outer[None], out_ref.shape)


def grad_kernel(logit_ref, lse_ref, tgt_ref, keep_ref, pan_ref, out_ref, grad):
    @pl.when(pl.program_id(0) == 0)
    def _():
        cols = lax.broadcasted_iota(jnp.int32, logit_ref.shape, 0)
        hot = cols == tgt_ref[...] - lax.axis_index("voc") * logit_ref.shape[0]
        soft = jnp.exp(logit_ref[...] - lse_ref[...])
        keep = keep_ref[...].astype(F32)
        grad[...] = ((soft - hot.astype(F32)) * keep).astype(BF16)

    out_ref[...] = jnp.dot(pan_ref[...], grad[...], preferred_element_type=F32).astype(BF16)


def total_kernel(parts_ref, out_ref):
    def add(k, total):
        return total + parts_ref[k].astype(F32)

    devices = parts_ref.shape[0]
    total = lax.fori_loop(1, devices, add, parts_ref[0].astype(F32), unroll=4)
    out_ref[...] = total.astype(BF16)


def scores_kernel(outer_ref, inner_ref, store_ref, out_ref, query, wide, *sums):
    groups, rank, tokens = outer_ref.shape
    half = rank // 2
    low = lax.broadcasted_iota(jnp.int32, (8, 128), 1) < rank
    eight = lax.broadcasted_iota(jnp.int32, (8, tokens), 0).astype(F32)

    def multiply(k, even_ref, odd_ref):
        span = inner_ref[k, rank:, :].astype(F32)
        block = jnp.floor(span * 0.125)
        row = (span - 8.0 * block)[0:8, :]
        mask = (row == eight).astype(F32)
        for c in (0, 1):
            wide[c] = inner_ref[k, 0:rank, 128 * c : 128 * (c + 1)].astype(F32)
        outer = outer_ref[k]
        shares = []
        for j in range(4):
            chosen = (block == float(j)).astype(F32).astype(BF16)
            shares.append(outer * jnp.concatenate([chosen] * (rank // 16), axis=0))
        for ref, side, order in ((even_ref, 0, (0, 1, 2, 3)), (odd_ref, 1, (1, 0, 3, 2))):
            columns = []
            for c in (0, 1):
                part = mask[:, 128 * c : 128 * (c + 1)]
                rows = [wide[c, pl.ds(2 * p + side, 8, stride=0), :] * part for p in range(half)]
                columns.append(jnp.concatenate(rows, axis=0).astype(BF16))
            left = jnp.concatenate(columns, axis=1)
            right = jnp.concatenate([shares[j] for j in order], axis=0)
            ref[...] = lax.dot_general(left, right, LANES_BOTH, preferred_element_type=F32)

    def arrange(k, even_ref, odd_ref):
        base = pl.multiple_of(k * SPAN_DEV, SPAN_DEV)
        for pair in range(half):
            for c in (0, 1):
                x = even_ref[8 * pair : 8 * (pair + 1), 128 * c : 128 * (c + 1)]
                y = odd_ref[8 * pair : 8 * (pair + 1), 128 * c : 128 * (c + 1)]
                straight = jnp.where(low, x, y)
                crossed = pltpu.roll(jnp.where(low, y, x), rank, axis=1)
                query[pl.ds(base + 16 * c, 16), 128 * pair : 128 * (pair + 1)] = (
                    jnp.concatenate([straight, crossed], axis=0).astype(BF16)
                )

    first, second = sums[0:2], sums[2:4]

    def both(step, carry):
        multiply(2 * step, *first)
        arrange(lax.rem(2 * step + groups - 1, groups), *second)
        multiply(2 * step + 1, *second)
        arrange(2 * step, *first)
        return carry

    lax.fori_loop(0, groups // 2, both, 0)
    arrange(groups - 1, *second)

    result = lax.dot_general(query[...], store_ref[...], LANES_BOTH, preferred_element_type=F32)
    out_ref[...] = result * (1.0 / RANK)


def body(hidden, panel, in_proj, out_proj, targets, keep, span_ids, store):
    tokens, width = hidden.shape
    cols = panel.shape[1]
    devices = lax.axis_size("voc")
    share = width // devices
    steps = 4
    piece = width // steps
    one = lambda i: (0, 0)
    logit, msg, inner = call(
        functools.partial(logits_kernel, steps),
        (
            jax.ShapeDtypeStruct((cols, tokens), F32),
            jax.ShapeDtypeStruct((devices, 8, tokens), F32),
            jax.ShapeDtypeStruct((RANK + 16, tokens), BF16),
        ),
        grid_spec=pltpu.PrefetchScalarGridSpec(
            num_scalar_prefetch=0,
            grid=(steps,),
            in_specs=[
                pl.BlockSpec((tokens, piece), lambda i: (0, i)),
                pl.BlockSpec((piece, cols), lambda i: (i, 0)),
                pl.BlockSpec((RANK, piece), lambda i: (0, i)),
                pl.BlockSpec((RANK, cols), one),
                pl.BlockSpec((1, tokens), one),
                pl.BlockSpec((1, tokens), one),
            ],
            out_specs=[
                pl.BlockSpec((cols, tokens), one),
                pl.BlockSpec((devices, 8, tokens), lambda i: (0, 0, 0)),
                pl.BlockSpec((RANK + 16, tokens), one),
            ],
            scratch_shapes=[
                pltpu.VMEM((tokens, cols), F32),
                pltpu.VMEM((RANK, tokens), F32),
                pltpu.VMEM((2 * RANK, tokens), F32),
            ],
        ),
        name="logits",
    )(hidden, panel, in_proj.T, out_proj.T, targets[None], span_ids[None])
    with jax.named_scope("stats_move"):
        got = lax.all_to_all(msg, "voc", 0, 0, tiled=True)
    with jax.named_scope("inner_move"):
        all_inner = lax.all_gather(inner, "tok", axis=0)
    got, all_inner = lax.optimization_barrier((got, all_inner))
    outer, lse = call(
        combine_kernel,
        (
            jax.ShapeDtypeStruct((devices, 2, tokens), BF16),
            jax.ShapeDtypeStruct((1, tokens), F32),
        ),
        in_specs=vmem(2),
        out_specs=tuple(vmem(2)),
        scratch_shapes=[pltpu.VMEM((devices, tokens), F32)],
        name="combine",
    )(resident(got), keep[None])
    with jax.named_scope("outer_move"):
        outer = lax.all_to_all(outer, "voc", 0, 0, tiled=True)
    blocks = 4
    partial = call(
        grad_kernel,
        jax.ShapeDtypeStruct((width, tokens), BF16),
        grid=(blocks,),
        in_specs=[
            pl.BlockSpec((cols, tokens), one),
            pl.BlockSpec((1, tokens), one),
            pl.BlockSpec((1, tokens), one),
            pl.BlockSpec((1, tokens), one),
            pl.BlockSpec((width // blocks, cols), lambda i: (i, 0)),
        ],
        out_specs=pl.BlockSpec((width // blocks, tokens), lambda i: (i, 0)),
        scratch_shapes=[pltpu.VMEM((cols, tokens), BF16)],
        name="grad",
    )(logit, lse, targets[None], keep[None], panel)
    partial = partial.reshape(devices, share, tokens)
    outer, partial = lax.optimization_barrier((outer, partial))
    with jax.named_scope("hidden_move"):
        parts = lax.all_to_all(partial, "voc", 0, 0, tiled=True)
    with jax.named_scope("gather_move"):
        all_outer = lax.all_gather(outer.reshape(RANK, tokens), "tok", axis=0)
    groups = all_outer.shape[0]
    scores = call(
        scores_kernel,
        jax.ShapeDtypeStruct((groups * SPAN_DEV, store.shape[0]), F32),
        in_specs=vmem(3),
        out_specs=vmem(1)[0],
        scratch_shapes=[pltpu.VMEM((groups * SPAN_DEV, RANK * RANK), BF16)]
        + [pltpu.VMEM((2, RANK, 128), F32)]
        + [pltpu.VMEM((RANK * 4, RANK * 4), F32)] * 4,
        name="scores",
    )(resident(all_outer), resident(all_inner), resident(store))
    hidden_grad = call(
        total_kernel,
        jax.ShapeDtypeStruct((share, tokens), BF16),
        in_specs=vmem(1),
        out_specs=vmem(1)[0],
        name="total",
    )(resident(parts)).T
    return (hidden_grad, scores)


def solution(mesh):
    placed = (
        P("tok", None),
        P(None, "voc"),
        P(),
        P("voc", None),
        P("tok"),
        P("tok"),
        P("tok"),
        P(("tok", "voc"), None),
    )
    return jax.shard_map(
        body,
        mesh=mesh,
        in_specs=placed,
        out_specs=(P("tok", "voc"), P(None, ("tok", "voc"))),
        check_vma=False,
    )
```

```python
import functools

import jax
import jax.numpy as jnp
from jax import lax
from jax.experimental import pallas as pl
from jax.experimental.pallas import tpu as pltpu
from jax.sharding import PartitionSpec as P

RANK = 64
SPAN_DEV = 32
LOW = -1e30
F32 = jnp.float32
BF16 = jnp.bfloat16
LANES_BOTH = (((1,), (1,)), ((), ()))


def resident(array):
    return pltpu.with_memory_space_constraint(array, pltpu.VMEM)


def call(kernel, out_shape, **kw):
    room = pltpu.CompilerParams(vmem_limit_bytes=16 << 20)
    return pl.pallas_call(kernel, out_shape=out_shape, compiler_params=room, **kw)


def vmem(n):
    return [pl.BlockSpec(memory_space=pltpu.VMEM)] * n


def pieces(x, count):
    found = []
    for _ in range(count):
        found.append(x.astype(BF16))
        x = x - found[-1].astype(F32)
    return found


def logits_kernel(classes, hid_ref, pan_ref, inp_ref, outp_ref, tgt_ref, span_ref,
                  logit_ref, msg_ref, inner_ref,
                  hid, pan, inp, outp, tgt, span, acc, acc_in, sems):
    steps, tokens, piece = hid.shape
    small = [
        pltpu.make_async_copy(a, b, sems.at[2 * steps + k])
        for k, (a, b) in enumerate(((inp_ref, inp), (outp_ref, outp), (tgt_ref, tgt), (span_ref, span)))
    ]
    left = [
        pltpu.make_async_copy(hid_ref.at[:, piece * i : piece * (i + 1)], hid.at[i], sems.at[i])
        for i in range(steps)
    ]
    right = [
        pltpu.make_async_copy(
            pan_ref.at[piece * i : piece * (i + 1), :], pan.at[i], sems.at[steps + i]
        )
        for i in range(steps)
    ]
    for i in range(steps):
        left[i].start()
        right[i].start()
        if i == 0:
            small[0].start()
    for copy in small[1:]:
        copy.start()
    for i in range(steps):
        left[i].wait()
        right[i].wait()
        if i == 0:
            small[0].wait()
        part = jnp.dot(hid[i], pan[i], preferred_element_type=F32)
        part_in = lax.dot_general(
            inp[:, piece * i : piece * (i + 1)], hid[i], LANES_BOTH, preferred_element_type=F32
        )
        if i == 0:
            acc[...] = part
            acc_in[...] = part_in
        else:
            acc[...] += part
            acc_in[...] += part_in
    for copy in small[1:]:
        copy.wait()
    inner_ref[0:RANK, :] = acc_in[...].astype(BF16)
    local = (span[...] - lax.axis_index("tok") * SPAN_DEV).astype(F32)
    inner_ref[RANK:, :] = jnp.broadcast_to(local, (16, tokens)).astype(BF16)
    logit = acc[...].T
    logit_ref[...] = logit
    cols = lax.broadcasted_iota(jnp.int32, logit.shape, 0)
    hot = cols == tgt[...] - lax.axis_index("voc") * logit.shape[0]
    others = jnp.where(hot, LOW, logit)
    top = jnp.max(others, axis=0, keepdims=True)
    weight = jnp.exp(others - top)
    total = jnp.sum(weight, axis=0, keepdims=True)
    own = jnp.max(jnp.where(hot, logit, LOW), axis=0, keepdims=True)
    proj = outp[...]
    soft = jnp.dot(proj, weight.astype(BF16), preferred_element_type=F32).astype(BF16)
    picked = jnp.dot(proj, hot.astype(F32).astype(BF16), preferred_element_type=F32).astype(BF16)
    stats = pieces(top, 3) + pieces(total, 2) + pieces(own, 3)
    stats = jnp.concatenate([x.astype(F32) for x in stats], axis=0).astype(BF16)
    devices = msg_ref.shape[0]
    peers = devices // classes
    share = RANK // classes
    for w in range(devices):
        at = share * (w // peers)
        msg_ref[w, 0:share, :] = soft[at : at + share, :]
        msg_ref[w, share : 2 * share, :] = picked[at : at + share, :]
        msg_ref[w, 2 * share :, :] = stats


def combine_kernel(got_ref, keep_ref, out_ref, lse_ref, stat):
    devices, height, tokens = got_ref.shape
    share = (height - 8) // 2
    for v in range(devices):
        rows = got_ref[v, 2 * share :, :].astype(F32)
        stat[0, v : v + 1, :] = rows[0:1, :] + rows[1:2, :] + rows[2:3, :]
        stat[1, v : v + 1, :] = rows[3:4, :] + rows[4:5, :]
        stat[2, v : v + 1, :] = rows[5:6, :] + rows[6:7, :] + rows[7:8, :]
    tops = stat[0]
    own = jnp.max(stat[2], axis=0, keepdims=True)
    top = jnp.maximum(jnp.max(tops, axis=0, keepdims=True), own)
    scale = jnp.exp(tops - top)
    rest = jnp.sum(scale * stat[1], axis=0, keepdims=True)
    total = rest + jnp.exp(own - top)
    lse_ref[...] = top + jnp.log(total)
    keep = keep_ref[...].astype(F32)
    stat[0] = scale * (keep / total)
    gone = keep * (rest / total)
    part = jnp.zeros((share, tokens), F32)
    hot = jnp.zeros((share, tokens), F32)
    for v in range(devices):
        part += stat[0, v : v + 1, :] * got_ref[v, 0:share, :].astype(F32)
        hot += got_ref[v, share : 2 * share, :].astype(F32)
    outer = (part - gone * hot).astype(BF16)
    for w in range(out_ref.shape[0]):
        out_ref[w] = outer


def grad_kernel(logit_ref, lse_ref, tgt_ref, keep_ref, pan_ref, out_ref, grad):
    @pl.when(pl.program_id(0) == 0)
    def _():
        cols = lax.broadcasted_iota(jnp.int32, logit_ref.shape, 0)
        hot = cols == tgt_ref[...] - lax.axis_index("voc") * logit_ref.shape[0]
        soft = jnp.exp(logit_ref[...] - lse_ref[...])
        keep = keep_ref[...].astype(F32)
        grad[...] = ((soft - hot.astype(F32)) * keep).astype(BF16)

    out_ref[...] = jnp.dot(pan_ref[...], grad[...], preferred_element_type=F32).astype(BF16)


def total_kernel(parts_ref, out_ref):
    def add(k, total):
        return total + parts_ref[k].astype(F32)

    devices = parts_ref.shape[0]
    total = lax.fori_loop(1, devices, add, parts_ref[0].astype(F32), unroll=4)
    out_ref[...] = total.astype(BF16)


def scores_kernel(outer_ref, inner_ref, store_hbm, out_ref, query, wide, store_ref, sem, *sums):
    groups, rank, tokens = outer_ref.shape
    half = rank // 2
    low = lax.broadcasted_iota(jnp.int32, (8, 128), 1) < rank
    eight = lax.broadcasted_iota(jnp.int32, (8, tokens), 0).astype(F32)

    def multiply(k, even_ref, odd_ref):
        span = inner_ref[k, rank:, :].astype(F32)
        block = jnp.floor(span * 0.125)
        row = (span - 8.0 * block)[0:8, :]
        mask = (row == eight).astype(F32)
        for c in (0, 1):
            wide[c] = inner_ref[k, 0:rank, 128 * c : 128 * (c + 1)].astype(F32)
        outer = outer_ref[k]
        shares = []
        for j in range(4):
            chosen = (block == float(j)).astype(F32).astype(BF16)
            shares.append(outer * jnp.concatenate([chosen] * (rank // 16), axis=0))
        for ref, side, order in ((even_ref, 0, (0, 1, 2, 3)), (odd_ref, 1, (1, 0, 3, 2))):
            columns = []
            for c in (0, 1):
                part = mask[:, 128 * c : 128 * (c + 1)]
                rows = [wide[c, pl.ds(2 * p + side, 8, stride=0), :] * part for p in range(half)]
                columns.append(jnp.concatenate(rows, axis=0).astype(BF16))
            left = jnp.concatenate(columns, axis=1)
            right = jnp.concatenate([shares[j] for j in order], axis=0)
            ref[...] = lax.dot_general(left, right, LANES_BOTH, preferred_element_type=F32)

    def arrange(k, even_ref, odd_ref):
        base = pl.multiple_of(k * SPAN_DEV, SPAN_DEV)
        for pair in range(half):
            for c in (0, 1):
                x = even_ref[8 * pair : 8 * (pair + 1), 128 * c : 128 * (c + 1)]
                y = odd_ref[8 * pair : 8 * (pair + 1), 128 * c : 128 * (c + 1)]
                straight = jnp.where(low, x, y)
                crossed = pltpu.roll(jnp.where(low, y, x), rank, axis=1)
                query[pl.ds(base + 16 * c, 16), 128 * pair : 128 * (pair + 1)] = (
                    jnp.concatenate([straight, crossed], axis=0).astype(BF16)
                )

    first, second = sums[0:2], sums[2:4]
    fetch = pltpu.make_async_copy(store_hbm, store_ref, sem)
    fetch.start()

    def both(step, carry):
        multiply(2 * step, *first)
        arrange(lax.rem(2 * step + groups - 1, groups), *second)
        multiply(2 * step + 1, *second)
        arrange(2 * step, *first)
        return carry

    lax.fori_loop(0, groups // 2, both, 0)
    arrange(groups - 1, *second)

    fetch.wait()
    result = lax.dot_general(query[...], store_ref[...], LANES_BOTH, preferred_element_type=F32)
    out_ref[...] = result * (1.0 / RANK)


def body(hidden, panel, in_proj, out_proj, targets, keep, span_ids, store):
    tokens, width = hidden.shape
    cols = panel.shape[1]
    devices = lax.axis_size("voc")
    share = width // devices
    steps = 4
    piece = width // steps
    classes = 4
    height = 2 * RANK // classes + 8
    one = lambda i: (0, 0)
    inputs = (hidden, panel, in_proj.T, out_proj.T, targets[None], span_ids[None])
    logit, msg, inner = call(
        functools.partial(logits_kernel, classes),
        (
            jax.ShapeDtypeStruct((cols, tokens), F32),
            jax.ShapeDtypeStruct((devices, height, tokens), BF16),
            jax.ShapeDtypeStruct((RANK + 16, tokens), BF16),
        ),
        in_specs=[pl.BlockSpec(memory_space=pltpu.HBM)] * 6,
        out_specs=tuple(vmem(3)),
        scratch_shapes=[
            pltpu.VMEM((steps, tokens, piece), BF16),
            pltpu.VMEM((steps, piece, cols), BF16),
            pltpu.VMEM((RANK, width), BF16),
            pltpu.VMEM((RANK, cols), BF16),
            pltpu.VMEM((1, tokens), jnp.int32),
            pltpu.VMEM((1, tokens), jnp.int32),
            pltpu.VMEM((tokens, cols), F32),
            pltpu.VMEM((RANK, tokens), F32),
            pltpu.SemaphoreType.DMA((2 * steps + 4,)),
        ],
        name="logits",
    )(*(pltpu.with_memory_space_constraint(x, pltpu.HBM) for x in inputs))
    with jax.named_scope("stats_move"):
        got = lax.all_to_all(msg, "voc", 0, 0, tiled=True)
    with jax.named_scope("inner_move"):
        all_inner = lax.all_gather(inner, "tok", axis=0)
    got, all_inner = lax.optimization_barrier((got, all_inner))
    outer, lse = call(
        combine_kernel,
        (
            jax.ShapeDtypeStruct((classes, RANK // classes, tokens), BF16),
            jax.ShapeDtypeStruct((1, tokens), F32),
        ),
        in_specs=vmem(2),
        out_specs=tuple(vmem(2)),
        scratch_shapes=[pltpu.VMEM((3, devices, tokens), F32)],
        name="combine",
    )(resident(got), keep[None])
    with jax.named_scope("outer_move"):
        peers = devices // classes
        lines = [[z + peers * x for x in range(classes)] for z in range(peers)]
        outer = lax.all_to_all(outer, "voc", 0, 0, tiled=True, axis_index_groups=lines)
    blocks = 4
    partial = call(
        grad_kernel,
        jax.ShapeDtypeStruct((width, tokens), BF16),
        grid=(blocks,),
        in_specs=[
            pl.BlockSpec((cols, tokens), one),
            pl.BlockSpec((1, tokens), one),
            pl.BlockSpec((1, tokens), one),
            pl.BlockSpec((1, tokens), one),
            pl.BlockSpec((width // blocks, cols), lambda i: (i, 0)),
        ],
        out_specs=pl.BlockSpec((width // blocks, tokens), lambda i: (i, 0)),
        scratch_shapes=[pltpu.VMEM((cols, tokens), BF16)],
        name="grad",
    )(logit, lse, targets[None], keep[None], panel)
    partial = partial.reshape(devices, share, tokens)
    outer, partial = lax.optimization_barrier((outer, partial))
    with jax.named_scope("hidden_move"):
        parts = lax.all_to_all(partial, "voc", 0, 0, tiled=True)
    with jax.named_scope("gather_move"):
        all_outer = lax.all_gather(outer.reshape(RANK, tokens), "tok", axis=0)
    groups = all_outer.shape[0]
    scores = call(
        scores_kernel,
        jax.ShapeDtypeStruct((groups * SPAN_DEV, store.shape[0]), F32),
        in_specs=vmem(2) + [pl.BlockSpec(memory_space=pltpu.HBM)],
        out_specs=vmem(1)[0],
        scratch_shapes=[pltpu.VMEM((groups * SPAN_DEV, RANK * RANK), BF16)]
        + [pltpu.VMEM((2, RANK, 128), F32)]
        + [pltpu.VMEM(store.shape, BF16), pltpu.SemaphoreType.DMA]
        + [pltpu.VMEM((RANK * 4, RANK * 4), F32)] * 4,
        name="scores",
    )(resident(all_outer), resident(all_inner), pltpu.with_memory_space_constraint(store, pltpu.HBM))
    hidden_grad = call(
        total_kernel,
        jax.ShapeDtypeStruct((share, tokens), BF16),
        in_specs=vmem(1),
        out_specs=vmem(1)[0],
        name="total",
    )(resident(parts)).T
    return (hidden_grad, scores)


def solution(mesh):
    placed = (
        P("tok", None),
        P(None, "voc"),
        P(),
        P("voc", None),
        P("tok"),
        P("tok"),
        P("tok"),
        P(("tok", "voc"), None),
    )
    return jax.shard_map(
        body,
        mesh=mesh,
        in_specs=placed,
        out_specs=(P("tok", "voc"), P(None, ("tok", "voc"))),
        check_vma=False,
    )
```

```python
import functools

import jax
import jax.numpy as jnp
from jax import lax
from jax.experimental import pallas as pl
from jax.experimental.pallas import tpu as pltpu
from jax.sharding import PartitionSpec as P

RANK = 64
SPAN_DEV = 32
LOW = -1e30
F32 = jnp.float32
BF16 = jnp.bfloat16
LANES_BOTH = (((1,), (1,)), ((), ()))


def resident(array):
    return pltpu.with_memory_space_constraint(array, pltpu.VMEM)


def call(kernel, out_shape, **kw):
    room = pltpu.CompilerParams(vmem_limit_bytes=16 << 20)
    return pl.pallas_call(kernel, out_shape=out_shape, compiler_params=room, **kw)


def vmem(n):
    return [pl.BlockSpec(memory_space=pltpu.VMEM)] * n


def pieces(x, count):
    found = []
    for _ in range(count):
        found.append(x.astype(BF16))
        x = x - found[-1].astype(F32)
    return found


def logits_kernel(classes, hid_ref, pan_ref, inp_ref, outp_ref, tgt_ref, span_ref,
                  logit_ref, msg_ref, inner_ref,
                  hid, pan, inp, outp, tgt, span, acc, acc_in, sems):
    steps, tokens, piece = hid.shape
    small = [
        pltpu.make_async_copy(a, b, sems.at[2 * steps + k])
        for k, (a, b) in enumerate(((inp_ref, inp), (outp_ref, outp), (tgt_ref, tgt), (span_ref, span)))
    ]
    left = [
        pltpu.make_async_copy(hid_ref.at[:, piece * i : piece * (i + 1)], hid.at[i], sems.at[i])
        for i in range(steps)
    ]
    right = [
        pltpu.make_async_copy(
            pan_ref.at[piece * i : piece * (i + 1), :], pan.at[i], sems.at[steps + i]
        )
        for i in range(steps)
    ]
    for i in range(steps):
        left[i].start()
        right[i].start()
        if i == 0:
            small[0].start()
    for copy in small[1:]:
        copy.start()
    for i in range(steps):
        left[i].wait()
        right[i].wait()
        if i == 0:
            small[0].wait()
        part = jnp.dot(hid[i], pan[i], preferred_element_type=F32)
        part_in = lax.dot_general(
            inp[:, piece * i : piece * (i + 1)], hid[i], LANES_BOTH, preferred_element_type=F32
        )
        if i == 0:
            acc[...] = part
            acc_in[...] = part_in
        else:
            acc[...] += part
            acc_in[...] += part_in
    for copy in small[1:]:
        copy.wait()
    inner_ref[0:RANK, :] = acc_in[...].astype(BF16)
    local = (span[...] - lax.axis_index("tok") * SPAN_DEV).astype(F32)
    inner_ref[RANK:, :] = jnp.broadcast_to(local, (16, tokens)).astype(BF16)
    logit = acc[...].T
    logit_ref[...] = logit
    cols = lax.broadcasted_iota(jnp.int32, logit.shape, 0)
    hot = cols == tgt[...] - lax.axis_index("voc") * logit.shape[0]
    others = jnp.where(hot, LOW, logit)
    top = jnp.max(others, axis=0, keepdims=True)
    weight = jnp.exp(others - top)
    total = jnp.sum(weight, axis=0, keepdims=True)
    own = jnp.max(jnp.where(hot, logit, LOW), axis=0, keepdims=True)
    proj = outp[...]
    soft = jnp.dot(proj, weight.astype(BF16), preferred_element_type=F32).astype(BF16)
    picked = jnp.dot(proj, hot.astype(F32).astype(BF16), preferred_element_type=F32).astype(BF16)
    stats = pieces(top, 3) + pieces(total, 2) + pieces(own, 3)
    stats = jnp.concatenate([x.astype(F32) for x in stats], axis=0).astype(BF16)
    devices = msg_ref.shape[0]
    peers = devices // classes
    share = RANK // classes
    for w in range(devices):
        at = share * (w // peers)
        msg_ref[w, 0:share, :] = soft[at : at + share, :]
        msg_ref[w, share : 2 * share, :] = picked[at : at + share, :]
        msg_ref[w, 2 * share :, :] = stats


def combine_kernel(got_ref, logit_ref, tgt_ref, keep_ref, pan_ref, out_ref, stat, grad, chunk):
    devices, height, tokens = got_ref.shape
    share = (height - 8) // 2

    @pl.when(pl.program_id(0) == 0)
    def _():
        for v in range(devices):
            rows = got_ref[v, 2 * share :, :].astype(F32)
            stat[0, v : v + 1, :] = rows[0:1, :] + rows[1:2, :] + rows[2:3, :]
            stat[1, v : v + 1, :] = rows[3:4, :] + rows[4:5, :]
            stat[2, v : v + 1, :] = rows[5:6, :] + rows[6:7, :] + rows[7:8, :]
        tops = stat[0]
        own = jnp.max(stat[2], axis=0, keepdims=True)
        top = jnp.maximum(jnp.max(tops, axis=0, keepdims=True), own)
        scale = jnp.exp(tops - top)
        rest = jnp.sum(scale * stat[1], axis=0, keepdims=True)
        total = rest + jnp.exp(own - top)
        lse = top + jnp.log(total)
        keep = keep_ref[...].astype(F32)
        stat[0] = scale * (keep / total)
        gone = keep * (rest / total)
        cols = lax.broadcasted_iota(jnp.int32, logit_ref.shape, 0)
        hot = cols == tgt_ref[...] - lax.axis_index("voc") * logit_ref.shape[0]
        soft = jnp.exp(logit_ref[...] - lse)
        grad[...] = ((soft - hot.astype(F32)) * keep).astype(BF16)
        part = jnp.zeros((share, tokens), F32)
        picked = jnp.zeros((share, tokens), F32)
        for v in range(devices):
            part += stat[0, v : v + 1, :] * got_ref[v, 0:share, :].astype(F32)
            picked += got_ref[v, share : 2 * share, :].astype(F32)
        chunk[...] = (part - gone * picked).astype(BF16)

    out_ref[0, 0:share, :] = chunk[...]
    out_ref[0, share:, :] = jnp.dot(
        pan_ref[...], grad[...], preferred_element_type=F32
    ).astype(BF16)


def line_kernel(got_ref, outer_ref, sum_ref):
    classes, share, _ = outer_ref.shape
    for x in range(classes):
        outer_ref[x] = got_ref[x, 0:share, :]
    rows = sum_ref.shape[0]
    step = 64

    def add(k, carry):
        at = pl.multiple_of(k * step, step)
        total = got_ref[0, pl.ds(share + at, step), :].astype(F32)
        for x in range(1, classes):
            total += got_ref[x, pl.ds(share + at, step), :].astype(F32)
        sum_ref[pl.ds(at, step), :] = total.astype(BF16)
        return carry

    lax.fori_loop(0, rows // step, add, 0)


def total_kernel(parts_ref, out_ref):
    def add(k, total):
        return total + parts_ref[k].astype(F32)

    devices = parts_ref.shape[0]
    total = lax.fori_loop(1, devices, add, parts_ref[0].astype(F32), unroll=4)
    out_ref[...] = total.astype(BF16)


def scores_kernel(outer_ref, inner_ref, store_hbm, out_ref, query, wide, store_ref, sem, *sums):
    groups, rank, tokens = outer_ref.shape
    half = rank // 2
    low = lax.broadcasted_iota(jnp.int32, (8, 128), 1) < rank
    eight = lax.broadcasted_iota(jnp.int32, (8, tokens), 0).astype(F32)

    def multiply(k, even_ref, odd_ref):
        span = inner_ref[k, rank:, :].astype(F32)
        block = jnp.floor(span * 0.125)
        row = (span - 8.0 * block)[0:8, :]
        mask = (row == eight).astype(F32)
        for c in (0, 1):
            wide[c] = inner_ref[k, 0:rank, 128 * c : 128 * (c + 1)].astype(F32)
        outer = outer_ref[k]
        shares = []
        for j in range(4):
            chosen = (block == float(j)).astype(F32).astype(BF16)
            shares.append(outer * jnp.concatenate([chosen] * (rank // 16), axis=0))
        for ref, side, order in ((even_ref, 0, (0, 1, 2, 3)), (odd_ref, 1, (1, 0, 3, 2))):
            columns = []
            for c in (0, 1):
                part = mask[:, 128 * c : 128 * (c + 1)]
                rows = [wide[c, pl.ds(2 * p + side, 8, stride=0), :] * part for p in range(half)]
                columns.append(jnp.concatenate(rows, axis=0).astype(BF16))
            left = jnp.concatenate(columns, axis=1)
            right = jnp.concatenate([shares[j] for j in order], axis=0)
            ref[...] = lax.dot_general(left, right, LANES_BOTH, preferred_element_type=F32)

    def arrange(k, even_ref, odd_ref):
        base = pl.multiple_of(k * SPAN_DEV, SPAN_DEV)
        for pair in range(half):
            for c in (0, 1):
                x = even_ref[8 * pair : 8 * (pair + 1), 128 * c : 128 * (c + 1)]
                y = odd_ref[8 * pair : 8 * (pair + 1), 128 * c : 128 * (c + 1)]
                straight = jnp.where(low, x, y)
                crossed = pltpu.roll(jnp.where(low, y, x), rank, axis=1)
                query[pl.ds(base + 16 * c, 16), 128 * pair : 128 * (pair + 1)] = (
                    jnp.concatenate([straight, crossed], axis=0).astype(BF16)
                )

    first, second = sums[0:2], sums[2:4]
    fetch = pltpu.make_async_copy(store_hbm, store_ref, sem)
    fetch.start()

    def both(step, carry):
        multiply(2 * step, *first)
        arrange(lax.rem(2 * step + groups - 1, groups), *second)
        multiply(2 * step + 1, *second)
        arrange(2 * step, *first)
        return carry

    lax.fori_loop(0, groups // 2, both, 0)
    arrange(groups - 1, *second)

    fetch.wait()
    result = lax.dot_general(query[...], store_ref[...], LANES_BOTH, preferred_element_type=F32)
    out_ref[...] = result * (1.0 / RANK)


def body(hidden, panel, in_proj, out_proj, targets, keep, span_ids, store):
    tokens, width = hidden.shape
    cols = panel.shape[1]
    devices = lax.axis_size("voc")
    share = width // devices
    steps = 4
    piece = width // steps
    classes = 4
    height = 2 * RANK // classes + 8
    one = lambda i: (0, 0)
    inputs = (hidden, panel, in_proj.T, out_proj.T, targets[None], span_ids[None])
    logit, msg, inner = call(
        functools.partial(logits_kernel, classes),
        (
            jax.ShapeDtypeStruct((cols, tokens), F32),
            jax.ShapeDtypeStruct((devices, height, tokens), BF16),
            jax.ShapeDtypeStruct((RANK + 16, tokens), BF16),
        ),
        in_specs=[pl.BlockSpec(memory_space=pltpu.HBM)] * 6,
        out_specs=tuple(vmem(3)),
        scratch_shapes=[
            pltpu.VMEM((steps, tokens, piece), BF16),
            pltpu.VMEM((steps, piece, cols), BF16),
            pltpu.VMEM((RANK, width), BF16),
            pltpu.VMEM((RANK, cols), BF16),
            pltpu.VMEM((1, tokens), jnp.int32),
            pltpu.VMEM((1, tokens), jnp.int32),
            pltpu.VMEM((tokens, cols), F32),
            pltpu.VMEM((RANK, tokens), F32),
            pltpu.SemaphoreType.DMA((2 * steps + 4,)),
        ],
        name="logits",
    )(*(pltpu.with_memory_space_constraint(x, pltpu.HBM) for x in inputs))
    with jax.named_scope("stats_move"):
        got = lax.all_to_all(msg, "voc", 0, 0, tiled=True)
    with jax.named_scope("inner_move"):
        all_inner = lax.all_gather(inner, "tok", axis=0)
    got, all_inner = lax.optimization_barrier((got, all_inner))
    peers = devices // classes
    rows = width // classes
    mixed = call(
        combine_kernel,
        jax.ShapeDtypeStruct((classes, RANK // classes + rows, tokens), BF16),
        grid=(classes,),
        in_specs=[
            pl.BlockSpec((devices, height, tokens), lambda i: (0, 0, 0)),
            pl.BlockSpec((cols, tokens), one),
            pl.BlockSpec((1, tokens), one),
            pl.BlockSpec((1, tokens), one),
            pl.BlockSpec((rows, cols), lambda i: (i, 0)),
        ],
        out_specs=pl.BlockSpec((1, RANK // classes + rows, tokens), lambda i: (i, 0, 0)),
        scratch_shapes=[
            pltpu.VMEM((3, devices, tokens), F32),
            pltpu.VMEM((cols, tokens), BF16),
            pltpu.VMEM((RANK // classes, tokens), BF16),
        ],
        name="combine",
    )(resident(got), resident(logit), targets[None], keep[None], resident(panel))
    with jax.named_scope("mixed_move"):
        lines = [[z + peers * x for x in range(classes)] for z in range(peers)]
        mixed = lax.all_to_all(mixed, "voc", 0, 0, tiled=True, axis_index_groups=lines)
    outer, partial = call(
        line_kernel,
        (
            jax.ShapeDtypeStruct((classes, RANK // classes, tokens), BF16),
            jax.ShapeDtypeStruct((rows, tokens), BF16),
        ),
        in_specs=vmem(1),
        out_specs=tuple(vmem(2)),
        name="line",
    )(resident(mixed))
    with jax.named_scope("hidden_move"):
        planes = [[z + peers * x for z in range(peers)] for x in range(classes)]
        parts = lax.all_to_all(
            partial.reshape(peers, share, tokens), "voc", 0, 0, tiled=True, axis_index_groups=planes
        )
    with jax.named_scope("gather_move"):
        all_outer = lax.all_gather(outer.reshape(RANK, tokens), "tok", axis=0)
    groups = all_outer.shape[0]
    scores = call(
        scores_kernel,
        jax.ShapeDtypeStruct((groups * SPAN_DEV, store.shape[0]), F32),
        in_specs=vmem(2) + [pl.BlockSpec(memory_space=pltpu.HBM)],
        out_specs=vmem(1)[0],
        scratch_shapes=[pltpu.VMEM((groups * SPAN_DEV, RANK * RANK), BF16)]
        + [pltpu.VMEM((2, RANK, 128), F32)]
        + [pltpu.VMEM(store.shape, BF16), pltpu.SemaphoreType.DMA]
        + [pltpu.VMEM((RANK * 4, RANK * 4), F32)] * 4,
        name="scores",
    )(resident(all_outer), resident(all_inner), pltpu.with_memory_space_constraint(store, pltpu.HBM))
    hidden_grad = call(
        total_kernel,
        jax.ShapeDtypeStruct((share, tokens), BF16),
        in_specs=vmem(1),
        out_specs=vmem(1)[0],
        name="total",
    )(resident(parts)).T
    return (hidden_grad, scores)


def solution(mesh):
    placed = (
        P("tok", None),
        P(None, "voc"),
        P(),
        P("voc", None),
        P("tok"),
        P("tok"),
        P("tok"),
        P(("tok", "voc"), None),
    )
    return jax.shard_map(
        body,
        mesh=mesh,
        in_specs=placed,
        out_specs=(P("tok", "voc"), P(None, ("tok", "voc"))),
        check_vma=False,
    )
```

```python
import functools

import jax
import jax.numpy as jnp
from jax import lax
from jax.experimental import pallas as pl
from jax.experimental.pallas import tpu as pltpu
from jax.sharding import PartitionSpec as P


RANK = 64
SPAN_DEV = 32
LOW = -1e30
F32 = jnp.float32
BF16 = jnp.bfloat16
LANES_BOTH = (((1,), (1,)), ((), ()))


def resident(array):
    return pltpu.with_memory_space_constraint(array, pltpu.VMEM)


def call(kernel, out_shape, **kw):
    room = pltpu.CompilerParams(vmem_limit_bytes=16 << 20)
    return pl.pallas_call(kernel, out_shape=out_shape, compiler_params=room, **kw)


def vmem(n):
    return [pl.BlockSpec(memory_space=pltpu.VMEM)] * n


def pieces(x, count):
    found = []
    for _ in range(count):
        found.append(x.astype(BF16))
        x = x - found[-1].astype(F32)
    return found


def logits_kernel(classes, hid_ref, pan_ref, inp_ref, outp_ref, tgt_ref, span_ref,
                  logit_ref, msg_ref, inner_ref,
                  hid, pan, inp, outp, tgt, span, acc, acc_in, sems):
    steps, tokens, piece = hid.shape
    small = [
        pltpu.make_async_copy(a, b, sems.at[2 * steps + k])
        for k, (a, b) in enumerate(((inp_ref, inp), (outp_ref, outp), (tgt_ref, tgt), (span_ref, span)))
    ]
    left = [
        pltpu.make_async_copy(hid_ref.at[:, piece * i : piece * (i + 1)], hid.at[i], sems.at[i])
        for i in range(steps)
    ]
    right = [
        pltpu.make_async_copy(
            pan_ref.at[piece * i : piece * (i + 1), :], pan.at[i], sems.at[steps + i]
        )
        for i in range(steps)
    ]
    for i in range(steps):
        left[i].start()
        right[i].start()
        if i == 0:
            small[0].start()
    for copy in small[1:]:
        copy.start()
    for i in range(steps):
        left[i].wait()
        right[i].wait()
        if i == 0:
            small[0].wait()
        part = jnp.dot(hid[i], pan[i], preferred_element_type=F32)
        part_in = lax.dot_general(
            inp[:, piece * i : piece * (i + 1)], hid[i], LANES_BOTH, preferred_element_type=F32
        )
        if i == 0:
            acc[...] = part
            acc_in[...] = part_in
        else:
            acc[...] += part
            acc_in[...] += part_in
    for copy in small[1:]:
        copy.wait()
    inner_ref[0:RANK, :] = acc_in[...].astype(BF16)
    local = (span[...] - lax.axis_index("tok") * SPAN_DEV).astype(F32)
    inner_ref[RANK:, :] = jnp.broadcast_to(local, (8, tokens)).astype(BF16)
    logit = acc[...].T
    logit_ref[...] = logit
    cols = lax.broadcasted_iota(jnp.int32, logit.shape, 0)
    hot = cols == tgt[...] - lax.axis_index("voc") * logit.shape[0]
    others = jnp.where(hot, LOW, logit)
    top = jnp.max(others, axis=0, keepdims=True)
    weight = jnp.exp(others - top)
    total = jnp.sum(weight, axis=0, keepdims=True)
    own = jnp.max(jnp.where(hot, logit, LOW), axis=0, keepdims=True)
    proj = outp[...]
    soft = jnp.dot(proj, weight.astype(BF16), preferred_element_type=F32).astype(BF16)
    picked = jnp.dot(proj, hot.astype(F32).astype(BF16), preferred_element_type=F32).astype(BF16)
    stats = pieces(top, 3) + pieces(total, 2) + pieces(own, 3)
    stats = jnp.concatenate([x.astype(F32) for x in stats], axis=0).astype(BF16)
    devices = msg_ref.shape[0]
    peers = devices // classes
    share = RANK // classes
    for w in range(devices):
        at = share * (w // peers)
        msg_ref[w, 0:share, :] = soft[at : at + share, :]
        msg_ref[w, share : 2 * share, :] = picked[at : at + share, :]
        msg_ref[w, 2 * share :, :] = stats


def combine_kernel(got_ref, keep_ref, out_ref, lse_ref, stat):
    devices, height, tokens = got_ref.shape
    share = (height - 8) // 2
    for v in range(devices):
        rows = got_ref[v, 2 * share :, :].astype(F32)
        stat[0, v : v + 1, :] = rows[0:1, :] + rows[1:2, :] + rows[2:3, :]
        stat[1, v : v + 1, :] = rows[3:4, :] + rows[4:5, :]
        stat[2, v : v + 1, :] = rows[5:6, :] + rows[6:7, :] + rows[7:8, :]
    tops = stat[0]
    own = jnp.max(stat[2], axis=0, keepdims=True)
    top = jnp.maximum(jnp.max(tops, axis=0, keepdims=True), own)
    scale = jnp.exp(tops - top)
    rest = jnp.sum(scale * stat[1], axis=0, keepdims=True)
    total = rest + jnp.exp(own - top)
    lse_ref[...] = top + jnp.log(total)
    keep = keep_ref[...].astype(F32)
    stat[0] = scale * (keep / total)
    gone = keep * (rest / total)
    part = jnp.zeros((share, tokens), F32)
    hot = jnp.zeros((share, tokens), F32)
    for v in range(devices):
        part += stat[0, v : v + 1, :] * got_ref[v, 0:share, :].astype(F32)
        hot += got_ref[v, share : 2 * share, :].astype(F32)
    outer = (part - gone * hot).astype(BF16)
    out_ref[...] = outer


def grad_kernel(logit_ref, lse_ref, tgt_ref, keep_ref, pan_ref, out_ref, grad):
    @pl.when(pl.program_id(0) == 0)
    def _():
        cols = lax.broadcasted_iota(jnp.int32, logit_ref.shape, 0)
        hot = cols == tgt_ref[...] - lax.axis_index("voc") * logit_ref.shape[0]
        soft = jnp.exp(logit_ref[...] - lse_ref[...])
        keep = keep_ref[...].astype(F32)
        grad[...] = ((soft - hot.astype(F32)) * keep).astype(BF16)

    rows = out_ref.shape[0]
    at = pl.multiple_of(pl.program_id(0) * rows, rows)
    out_ref[...] = jnp.dot(
        pan_ref[pl.ds(at, rows), :], grad[...], preferred_element_type=F32
    ).astype(BF16)


def pair_kernel(own_ref, near_ref, out_ref):
    out_ref[0] = own_ref[...]
    out_ref[1] = near_ref[...]


def assemble_kernel(pair_ref, far_ref, out_ref):
    mine = lax.axis_index("voc") // 8
    out_ref[mine] = pair_ref[0]
    out_ref[mine ^ 1] = pair_ref[1]
    out_ref[mine ^ 3] = far_ref[0]
    out_ref[mine ^ 2] = far_ref[1]


def total_kernel(parts_ref, out_ref):
    def add(k, total):
        return total + parts_ref[k].astype(F32)

    devices = parts_ref.shape[0]
    total = lax.fori_loop(1, devices, add, parts_ref[0].astype(F32), unroll=4)
    out_ref[...] = total.astype(BF16)


def scores_kernel(outer_ref, inner_ref, store_hbm, out_ref, query, wide, store_ref, sem, *sums):
    groups, rank, tokens = outer_ref.shape
    half = rank // 2
    low = lax.broadcasted_iota(jnp.int32, (8, 128), 1) < rank
    eight = lax.broadcasted_iota(jnp.int32, (8, tokens), 0).astype(F32)

    def multiply(k, even_ref, odd_ref):
        span = inner_ref[k, rank:, :].astype(F32)
        block = jnp.floor(span * 0.125)
        row = span - 8.0 * block
        mask = (row == eight).astype(F32)
        mask = jnp.concatenate([mask, mask], axis=0).astype(BF16)
        for c in (0, 1):
            wide[c] = inner_ref[k, 0:rank, 128 * c : 128 * (c + 1)].astype(F32)
        outer = outer_ref[k]
        shares = []
        for j in range(4):
            chosen = (block == float(j)).astype(F32)
            chosen = jnp.concatenate([chosen, chosen], axis=0).astype(BF16)
            shares.append(outer * jnp.concatenate([chosen] * (rank // 16), axis=0))
        for ref, side, order in ((even_ref, 0, (0, 1, 2, 3)), (odd_ref, 1, (1, 0, 3, 2))):
            columns = []
            for c in (0, 1):
                part = mask[:, 128 * c : 128 * (c + 1)]
                rows = [wide[c, pl.ds(2 * p + side, 8, stride=0), :] for p in range(half)]
                pairs = [jnp.concatenate(rows[p : p + 2], axis=0).astype(BF16) for p in range(0, half, 2)]
                columns.append(jnp.concatenate([x * part for x in pairs], axis=0))
            left = jnp.concatenate(columns, axis=1)
            right = jnp.concatenate([shares[j] for j in order], axis=0)
            ref[...] = lax.dot_general(left, right, LANES_BOTH, preferred_element_type=F32)

    def arrange(k, even_ref, odd_ref):
        base = pl.multiple_of(k * SPAN_DEV, SPAN_DEV)
        for pair in range(half):
            for c in (0, 1):
                x = even_ref[8 * pair : 8 * (pair + 1), 128 * c : 128 * (c + 1)]
                y = odd_ref[8 * pair : 8 * (pair + 1), 128 * c : 128 * (c + 1)]
                straight = jnp.where(low, x, y)
                crossed = pltpu.roll(jnp.where(low, y, x), rank, axis=1)
                query[pl.ds(base + 16 * c, 16), 128 * pair : 128 * (pair + 1)] = (
                    jnp.concatenate([straight, crossed], axis=0).astype(BF16)
                )

    first, second = sums[0:2], sums[2:4]
    fetch = pltpu.make_async_copy(store_hbm, store_ref, sem)
    fetch.start()

    def both(step, carry):
        for k in range(4):
            now, before = (first, second) if k % 2 == 0 else (second, first)
            multiply(4 * step + k, *now)
            arrange(lax.rem(4 * step + k + groups - 1, groups), *before)
        return carry

    lax.fori_loop(0, groups // 4, both, 0)
    arrange(groups - 1, *second)

    fetch.wait()
    result = lax.dot_general(query[...], store_ref[...], LANES_BOTH, preferred_element_type=F32)
    out_ref[...] = result * (1.0 / RANK)


def body(hidden, panel, in_proj, out_proj, targets, keep, span_ids, store):
    tokens, width = hidden.shape
    cols = panel.shape[1]
    devices = lax.axis_size("voc")
    share = width // devices
    steps = 4
    piece = width // steps
    classes = 4
    height = 2 * RANK // classes + 8
    inputs = (hidden, panel, in_proj.T, out_proj.T, targets[None], span_ids[None])
    logit, msg, inner = call(
        functools.partial(logits_kernel, classes),
        (
            jax.ShapeDtypeStruct((cols, tokens), F32),
            jax.ShapeDtypeStruct((devices, height, tokens), BF16),
            jax.ShapeDtypeStruct((RANK + 8, tokens), BF16),
        ),
        in_specs=[pl.BlockSpec(memory_space=pltpu.HBM)] * 6,
        out_specs=tuple(vmem(3)),
        scratch_shapes=[
            pltpu.VMEM((steps, tokens, piece), BF16),
            pltpu.VMEM((steps, piece, cols), BF16),
            pltpu.VMEM((RANK, width), BF16),
            pltpu.VMEM((RANK, cols), BF16),
            pltpu.VMEM((1, tokens), jnp.int32),
            pltpu.VMEM((1, tokens), jnp.int32),
            pltpu.VMEM((tokens, cols), F32),
            pltpu.VMEM((RANK, tokens), F32),
            pltpu.SemaphoreType.DMA((2 * steps + 4,)),
        ],
        name="logits",
    )(*(pltpu.with_memory_space_constraint(x, pltpu.HBM) for x in inputs))
    got = lax.all_to_all(msg, "voc", 0, 0, tiled=True)
    all_inner = lax.all_gather(inner, "tok", axis=0)
    got, all_inner = lax.optimization_barrier((got, all_inner))
    outer, lse = call(
        combine_kernel,
        (
            jax.ShapeDtypeStruct((RANK // classes, tokens), BF16),
            jax.ShapeDtypeStruct((1, tokens), F32),
        ),
        in_specs=vmem(2),
        out_specs=tuple(vmem(2)),
        scratch_shapes=[pltpu.VMEM((3, devices, tokens), F32)],
        name="combine",
    )(resident(got), keep[None])
    near = lax.ppermute(outer, "voc", [(v, v ^ 8) for v in range(devices)])
    blocks = 4
    partial = call(
        grad_kernel,
        jax.ShapeDtypeStruct((width, tokens), BF16),
        grid=(blocks,),
        in_specs=vmem(5),
        out_specs=pl.BlockSpec((width // blocks, tokens), lambda i: (i, 0)),
        scratch_shapes=[pltpu.VMEM((cols, tokens), BF16)],
        name="grad",
    )(resident(logit), resident(lse), targets[None], keep[None], resident(panel))
    partial = partial.reshape(devices, share, tokens)
    parts = lax.all_to_all(partial, "voc", 0, 0, tiled=True)
    pair = call(
        pair_kernel,
        jax.ShapeDtypeStruct((2, RANK // classes, tokens), BF16),
        in_specs=vmem(2),
        out_specs=vmem(1)[0],
        name="pair",
    )(resident(outer), resident(near))
    far = lax.ppermute(pair, "voc", [(v, v ^ 24) for v in range(devices)])
    outer = call(
        assemble_kernel,
        jax.ShapeDtypeStruct((classes, RANK // classes, tokens), BF16),
        in_specs=vmem(2),
        out_specs=vmem(1)[0],
        name="assemble",
    )(resident(pair), resident(far))
    all_outer = lax.all_gather(outer.reshape(RANK, tokens), "tok", axis=0)
    groups = all_outer.shape[0]
    scores = call(
        scores_kernel,
        jax.ShapeDtypeStruct((groups * SPAN_DEV, store.shape[0]), F32),
        in_specs=vmem(2) + [pl.BlockSpec(memory_space=pltpu.HBM)],
        out_specs=vmem(1)[0],
        scratch_shapes=[pltpu.VMEM((groups * SPAN_DEV, RANK * RANK), BF16)]
        + [pltpu.VMEM((2, RANK, 128), F32)]
        + [pltpu.VMEM(store.shape, BF16), pltpu.SemaphoreType.DMA]
        + [pltpu.VMEM((RANK * 4, RANK * 4), F32)] * 4,
        name="scores",
    )(resident(all_outer), resident(all_inner), pltpu.with_memory_space_constraint(store, pltpu.HBM))
    hidden_grad = call(
        total_kernel,
        jax.ShapeDtypeStruct((share, tokens), BF16),
        in_specs=vmem(1),
        out_specs=vmem(1)[0],
        name="total",
    )(resident(parts)).T
    return (hidden_grad, scores)


def solution(mesh):
    placed = (
        P("tok", None),
        P(None, "voc"),
        P(),
        P("voc", None),
        P("tok"),
        P("tok"),
        P("tok"),
        P(("tok", "voc"), None),
    )

    return jax.shard_map(
        body,
        mesh=mesh,
        in_specs=placed,
        out_specs=(P("tok", "voc"), P(None, ("tok", "voc"))),
        check_vma=False,
    )
```

```python
import functools

import jax
import jax.numpy as jnp
from jax import lax
from jax.experimental import pallas as pl
from jax.experimental.pallas import tpu as pltpu
from jax.sharding import PartitionSpec as P


RANK = 64
SPAN_DEV = 32
LOW = -1e30
F32 = jnp.float32
BF16 = jnp.bfloat16
LANES_BOTH = (((1,), (1,)), ((), ()))


def resident(array):
    return pltpu.with_memory_space_constraint(array, pltpu.VMEM)


def call(kernel, out_shape, **kw):
    room = pltpu.CompilerParams(vmem_limit_bytes=16 << 20)
    return pl.pallas_call(kernel, out_shape=out_shape, compiler_params=room, **kw)


def vmem(n):
    return [pl.BlockSpec(memory_space=pltpu.VMEM)] * n


def pieces(x, count):
    found = []
    for _ in range(count):
        found.append(x.astype(BF16))
        x = x - found[-1].astype(F32)
    return found


def logits_kernel(classes, hid_ref, pan_ref, inp_ref, outp_ref, tgt_ref, span_ref,
                  logit_ref, msg_ref, inner_ref,
                  hid, pan, inp, outp, tgt, span, acc, acc_in, sems):
    steps, tokens, piece = hid.shape
    small = [
        pltpu.make_async_copy(a, b, sems.at[2 * steps + k])
        for k, (a, b) in enumerate(((inp_ref, inp), (outp_ref, outp), (tgt_ref, tgt), (span_ref, span)))
    ]
    left = [
        pltpu.make_async_copy(hid_ref.at[:, piece * i : piece * (i + 1)], hid.at[i], sems.at[i])
        for i in range(steps)
    ]
    right = [
        pltpu.make_async_copy(
            pan_ref.at[piece * i : piece * (i + 1), :], pan.at[i], sems.at[steps + i]
        )
        for i in range(steps)
    ]
    for i in range(steps):
        left[i].start()
        right[i].start()
        if i == 0:
            small[0].start()
    for copy in small[1:]:
        copy.start()
    for i in range(steps):
        left[i].wait()
        right[i].wait()
        if i == 0:
            small[0].wait()
        part = jnp.dot(hid[i], pan[i], preferred_element_type=F32)
        part_in = lax.dot_general(
            inp[:, piece * i : piece * (i + 1)], hid[i], LANES_BOTH, preferred_element_type=F32
        )
        if i == 0:
            acc[...] = part
            acc_in[...] = part_in
        else:
            acc[...] += part
            acc_in[...] += part_in
    for copy in small[1:]:
        copy.wait()
    inner_ref[0:RANK, :] = acc_in[...].astype(BF16)
    local = (span[...] - lax.axis_index("tok") * SPAN_DEV).astype(F32)
    inner_ref[RANK:, :] = jnp.broadcast_to(local, (8, tokens)).astype(BF16)
    logit = acc[...].T
    logit_ref[...] = logit
    cols = lax.broadcasted_iota(jnp.int32, logit.shape, 0)
    hot = cols == tgt[...] - lax.axis_index("voc") * logit.shape[0]
    others = jnp.where(hot, LOW, logit)
    top = jnp.max(others, axis=0, keepdims=True)
    weight = jnp.exp(others - top)
    total = jnp.sum(weight, axis=0, keepdims=True)
    own = jnp.max(jnp.where(hot, logit, LOW), axis=0, keepdims=True)
    proj = outp[...]
    soft = jnp.dot(proj, weight.astype(BF16), preferred_element_type=F32).astype(BF16)
    picked = jnp.dot(proj, hot.astype(F32).astype(BF16), preferred_element_type=F32).astype(BF16)
    stats = pieces(top, 3) + pieces(total, 2) + pieces(own, 3)
    stats = jnp.concatenate([x.astype(F32) for x in stats], axis=0).astype(BF16)
    devices = msg_ref.shape[0]
    peers = devices // classes
    share = RANK // classes
    for w in range(devices):
        at = share * (w // peers)
        msg_ref[w, 0:share, :] = soft[at : at + share, :]
        msg_ref[w, share : 2 * share, :] = picked[at : at + share, :]
        msg_ref[w, 2 * share :, :] = stats


def combine_kernel(got_ref, keep_ref, out_ref, lse_ref, stat):
    devices, height, tokens = got_ref.shape
    share = (height - 8) // 2
    for v in range(devices):
        rows = got_ref[v, 2 * share :, :].astype(F32)
        stat[0, v : v + 1, :] = rows[0:1, :] + rows[1:2, :] + rows[2:3, :]
        stat[1, v : v + 1, :] = rows[3:4, :] + rows[4:5, :]
        stat[2, v : v + 1, :] = rows[5:6, :] + rows[6:7, :] + rows[7:8, :]
    tops = stat[0]
    own = jnp.max(stat[2], axis=0, keepdims=True)
    top = jnp.maximum(jnp.max(tops, axis=0, keepdims=True), own)
    scale = jnp.exp(tops - top)
    rest = jnp.sum(scale * stat[1], axis=0, keepdims=True)
    total = rest + jnp.exp(own - top)
    lse_ref[...] = top + jnp.log(total)
    keep = keep_ref[...].astype(F32)
    stat[0] = scale * (keep / total)
    gone = keep * (rest / total)
    part = jnp.zeros((share, tokens), F32)
    hot = jnp.zeros((share, tokens), F32)
    for v in range(devices):
        part += stat[0, v : v + 1, :] * got_ref[v, 0:share, :].astype(F32)
        hot += got_ref[v, share : 2 * share, :].astype(F32)
    outer = (part - gone * hot).astype(BF16)
    out_ref[...] = outer


def grad_kernel(logit_ref, lse_ref, tgt_ref, keep_ref, pan_ref, out_ref, made, sems):
    cols = lax.broadcasted_iota(jnp.int32, logit_ref.shape, 0)
    hot = cols == tgt_ref[...] - lax.axis_index("voc") * logit_ref.shape[0]
    soft = jnp.exp(logit_ref[...] - lse_ref[...])
    keep = keep_ref[...].astype(F32)
    grad = ((soft - hot.astype(F32)) * keep).astype(BF16)
    blocks = sems.shape[0]
    rows = made.shape[0] // blocks
    copies = []
    for i in range(blocks):
        at = slice(rows * i, rows * (i + 1))
        made[at, :] = jnp.dot(pan_ref[at, :], grad, preferred_element_type=F32).astype(BF16)
        copies.append(pltpu.make_async_copy(made.at[at, :], out_ref.at[at, :], sems.at[i]))
        copies[-1].start()
    for copy in copies:
        copy.wait()


def pair_kernel(own_ref, near_ref, out_ref):
    out_ref[0] = own_ref[...]
    out_ref[1] = near_ref[...]


def assemble_kernel(pair_ref, far_ref, out_ref):
    mine = lax.axis_index("voc") // 8
    out_ref[mine] = pair_ref[0]
    out_ref[mine ^ 1] = pair_ref[1]
    out_ref[mine ^ 3] = far_ref[0]
    out_ref[mine ^ 2] = far_ref[1]


def total_kernel(parts_ref, out_ref):
    def add(k, total):
        return total + parts_ref[k].astype(F32)

    devices = parts_ref.shape[0]
    total = lax.fori_loop(1, devices, add, parts_ref[0].astype(F32), unroll=4)
    out_ref[...] = total.astype(BF16)


def scores_kernel(outer_ref, inner_ref, store_hbm, out_ref, query, wide, store_ref, sem, *sums):
    groups, rank, tokens = outer_ref.shape
    half = rank // 2
    low = lax.broadcasted_iota(jnp.int32, (8, 128), 1) < rank
    eight = lax.broadcasted_iota(jnp.int32, (8, tokens), 0).astype(F32)

    def multiply(k, even_ref, odd_ref):
        span = inner_ref[k, rank:, :].astype(F32)
        block = jnp.floor(span * 0.125)
        row = span - 8.0 * block
        mask = (row == eight).astype(F32)
        mask = jnp.concatenate([mask, mask], axis=0).astype(BF16)
        for c in (0, 1):
            wide[c] = inner_ref[k, 0:rank, 128 * c : 128 * (c + 1)].astype(F32)
        outer = outer_ref[k]
        shares = []
        for j in range(4):
            chosen = (block == float(j)).astype(F32)
            chosen = jnp.concatenate([chosen, chosen], axis=0).astype(BF16)
            shares.append(outer * jnp.concatenate([chosen] * (rank // 16), axis=0))
        for ref, side, order in ((even_ref, 0, (0, 1, 2, 3)), (odd_ref, 1, (1, 0, 3, 2))):
            columns = []
            for c in (0, 1):
                part = mask[:, 128 * c : 128 * (c + 1)]
                rows = [wide[c, pl.ds(2 * p + side, 8, stride=0), :] for p in range(half)]
                pairs = [jnp.concatenate(rows[p : p + 2], axis=0).astype(BF16) for p in range(0, half, 2)]
                columns.append(jnp.concatenate([x * part for x in pairs], axis=0))
            left = jnp.concatenate(columns, axis=1)
            right = jnp.concatenate([shares[j] for j in order], axis=0)
            ref[...] = lax.dot_general(left, right, LANES_BOTH, preferred_element_type=F32)

    def arrange(k, even_ref, odd_ref):
        base = pl.multiple_of(k * SPAN_DEV, SPAN_DEV)
        for pair in range(half):
            for c in (0, 1):
                x = even_ref[8 * pair : 8 * (pair + 1), 128 * c : 128 * (c + 1)]
                y = odd_ref[8 * pair : 8 * (pair + 1), 128 * c : 128 * (c + 1)]
                straight = jnp.where(low, x, y)
                crossed = pltpu.roll(jnp.where(low, y, x), rank, axis=1)
                query[pl.ds(base + 16 * c, 16), 128 * pair : 128 * (pair + 1)] = (
                    jnp.concatenate([straight, crossed], axis=0).astype(BF16)
                )

    first, second = sums[0:2], sums[2:4]
    fetch = pltpu.make_async_copy(store_hbm, store_ref, sem)
    fetch.start()

    def both(step, carry):
        for k in range(8):
            now, before = (first, second) if k % 2 == 0 else (second, first)
            multiply(8 * step + k, *now)
            arrange(lax.rem(8 * step + k + groups - 1, groups), *before)
        return carry

    lax.fori_loop(0, groups // 8, both, 0)
    arrange(groups - 1, *second)

    fetch.wait()
    result = lax.dot_general(query[...], store_ref[...], LANES_BOTH, preferred_element_type=F32)
    out_ref[...] = result * (1.0 / RANK)


def body(hidden, panel, in_proj, out_proj, targets, keep, span_ids, store):
    tokens, width = hidden.shape
    cols = panel.shape[1]
    devices = lax.axis_size("voc")
    share = width // devices
    steps = 4
    piece = width // steps
    classes = 4
    height = 2 * RANK // classes + 8
    inputs = (hidden, panel, in_proj.T, out_proj.T, targets[None], span_ids[None])
    logit, msg, inner = call(
        functools.partial(logits_kernel, classes),
        (
            jax.ShapeDtypeStruct((cols, tokens), F32),
            jax.ShapeDtypeStruct((devices, height, tokens), BF16),
            jax.ShapeDtypeStruct((RANK + 8, tokens), BF16),
        ),
        in_specs=[pl.BlockSpec(memory_space=pltpu.HBM)] * 6,
        out_specs=tuple(vmem(3)),
        scratch_shapes=[
            pltpu.VMEM((steps, tokens, piece), BF16),
            pltpu.VMEM((steps, piece, cols), BF16),
            pltpu.VMEM((RANK, width), BF16),
            pltpu.VMEM((RANK, cols), BF16),
            pltpu.VMEM((1, tokens), jnp.int32),
            pltpu.VMEM((1, tokens), jnp.int32),
            pltpu.VMEM((tokens, cols), F32),
            pltpu.VMEM((RANK, tokens), F32),
            pltpu.SemaphoreType.DMA((2 * steps + 4,)),
        ],
        name="logits",
    )(*(pltpu.with_memory_space_constraint(x, pltpu.HBM) for x in inputs))
    got = lax.all_to_all(msg, "voc", 0, 0, tiled=True)
    all_inner = lax.all_gather(inner, "tok", axis=0)
    got, all_inner = lax.optimization_barrier((got, all_inner))
    outer, lse = call(
        combine_kernel,
        (
            jax.ShapeDtypeStruct((RANK // classes, tokens), BF16),
            jax.ShapeDtypeStruct((1, tokens), F32),
        ),
        in_specs=vmem(2),
        out_specs=tuple(vmem(2)),
        scratch_shapes=[pltpu.VMEM((3, devices, tokens), F32)],
        name="combine",
    )(resident(got), keep[None])
    near = lax.ppermute(outer, "voc", [(v, v ^ 8) for v in range(devices)])
    partial = call(
        grad_kernel,
        jax.ShapeDtypeStruct((width, tokens), BF16),
        in_specs=vmem(5),
        out_specs=pl.BlockSpec(memory_space=pltpu.HBM),
        scratch_shapes=[
            pltpu.VMEM((width, tokens), BF16),
            pltpu.SemaphoreType.DMA((8,)),
        ],
        name="grad",
    )(resident(logit), resident(lse), targets[None], keep[None], resident(panel))
    partial = partial.reshape(devices, share, tokens)
    parts = lax.all_to_all(partial, "voc", 0, 0, tiled=True)
    pair = call(
        pair_kernel,
        jax.ShapeDtypeStruct((2, RANK // classes, tokens), BF16),
        in_specs=vmem(2),
        out_specs=vmem(1)[0],
        name="pair",
    )(resident(outer), resident(near))
    far = lax.ppermute(pair, "voc", [(v, v ^ 24) for v in range(devices)])
    outer = call(
        assemble_kernel,
        jax.ShapeDtypeStruct((classes, RANK // classes, tokens), BF16),
        in_specs=vmem(2),
        out_specs=vmem(1)[0],
        name="assemble",
    )(resident(pair), resident(far))
    all_outer = lax.all_gather(outer.reshape(RANK, tokens), "tok", axis=0)
    groups = all_outer.shape[0]
    scores = call(
        scores_kernel,
        jax.ShapeDtypeStruct((groups * SPAN_DEV, store.shape[0]), F32),
        in_specs=vmem(2) + [pl.BlockSpec(memory_space=pltpu.HBM)],
        out_specs=vmem(1)[0],
        scratch_shapes=[pltpu.VMEM((groups * SPAN_DEV, RANK * RANK), BF16)]
        + [pltpu.VMEM((2, RANK, 128), F32)]
        + [pltpu.VMEM(store.shape, BF16), pltpu.SemaphoreType.DMA]
        + [pltpu.VMEM((RANK * 4, RANK * 4), F32)] * 4,
        name="scores",
    )(resident(all_outer), resident(all_inner), pltpu.with_memory_space_constraint(store, pltpu.HBM))
    hidden_grad = call(
        total_kernel,
        jax.ShapeDtypeStruct((share, tokens), BF16),
        in_specs=vmem(1),
        out_specs=vmem(1)[0],
        name="total",
    )(resident(parts)).T
    return (hidden_grad, scores)


def solution(mesh):
    placed = (
        P("tok", None),
        P(None, "voc"),
        P(),
        P("voc", None),
        P("tok"),
        P("tok"),
        P("tok"),
        P(("tok", "voc"), None),
    )

    return jax.shard_map(
        body,
        mesh=mesh,
        in_specs=placed,
        out_specs=(P("tok", "voc"), P(None, ("tok", "voc"))),
        check_vma=False,
    )
```

```python
import functools

import jax
import jax.numpy as jnp
from jax import lax
from jax.experimental import pallas as pl
from jax.experimental.pallas import tpu as pltpu
from jax.sharding import PartitionSpec as P


RANK = 64
SPAN_DEV = 32
LOW = -1e30
F32 = jnp.float32
BF16 = jnp.bfloat16
LANES_BOTH = (((1,), (1,)), ((), ()))


def resident(array):
    return pltpu.with_memory_space_constraint(array, pltpu.VMEM)


def call(kernel, out_shape, **kw):
    room = pltpu.CompilerParams(vmem_limit_bytes=16 << 20)
    return pl.pallas_call(kernel, out_shape=out_shape, compiler_params=room, **kw)


def vmem(n):
    return [pl.BlockSpec(memory_space=pltpu.VMEM)] * n


def pieces(x, count):
    found = []
    for _ in range(count):
        found.append(x.astype(BF16))
        x = x - found[-1].astype(F32)
    return found


def logits_kernel(classes, hid_ref, pan_ref, inp_ref, outp_ref, tgt_ref, span_ref,
                  logit_ref, msg_ref, inner_ref,
                  hid, pan, inp, outp, tgt, span, acc, acc_in, sems):
    steps, tokens, piece = hid.shape
    small = [
        pltpu.make_async_copy(a, b, sems.at[2 * steps + k])
        for k, (a, b) in enumerate(((inp_ref, inp), (outp_ref, outp), (tgt_ref, tgt), (span_ref, span)))
    ]
    left = [
        pltpu.make_async_copy(hid_ref.at[:, piece * i : piece * (i + 1)], hid.at[i], sems.at[i])
        for i in range(steps)
    ]
    right = [
        pltpu.make_async_copy(
            pan_ref.at[piece * i : piece * (i + 1), :], pan.at[i], sems.at[steps + i]
        )
        for i in range(steps)
    ]
    for i in range(steps):
        left[i].start()
        right[i].start()
        if i == 0:
            small[0].start()
    for copy in small[1:]:
        copy.start()
    for i in range(steps):
        left[i].wait()
        right[i].wait()
        if i == 0:
            small[0].wait()
        part = jnp.dot(hid[i], pan[i], preferred_element_type=F32)
        part_in = lax.dot_general(
            inp[:, piece * i : piece * (i + 1)], hid[i], LANES_BOTH, preferred_element_type=F32
        )
        if i == 0:
            acc[...] = part
            acc_in[...] = part_in
        else:
            acc[...] += part
            acc_in[...] += part_in
    for copy in small[1:]:
        copy.wait()
    inner_ref[0:RANK, :] = acc_in[...].astype(BF16)
    local = (span[...] - lax.axis_index("tok") * SPAN_DEV).astype(F32)
    inner_ref[RANK:, :] = jnp.broadcast_to(local, (8, tokens)).astype(BF16)
    logit = acc[...].T
    logit_ref[...] = logit
    cols = lax.broadcasted_iota(jnp.int32, logit.shape, 0)
    hot = cols == tgt[...] - lax.axis_index("voc") * logit.shape[0]
    others = jnp.where(hot, LOW, logit)
    top = jnp.max(others, axis=0, keepdims=True)
    weight = jnp.exp(others - top)
    total = jnp.sum(weight, axis=0, keepdims=True)
    own = jnp.max(jnp.where(hot, logit, LOW), axis=0, keepdims=True)
    proj = outp[...]
    soft = jnp.dot(proj, weight.astype(BF16), preferred_element_type=F32).astype(BF16)
    picked = jnp.dot(proj, hot.astype(F32).astype(BF16), preferred_element_type=F32).astype(BF16)
    stats = pieces(top, 3) + pieces(total, 2) + pieces(own, 3)
    stats = jnp.concatenate([x.astype(F32) for x in stats], axis=0).astype(BF16)
    devices = msg_ref.shape[0]
    share = RANK // classes
    for w in range(devices):
        at = share * (w % classes)
        msg_ref[w, 0:share, :] = soft[at : at + share, :]
        msg_ref[w, share : 2 * share, :] = picked[at : at + share, :]
        msg_ref[w, 2 * share :, :] = stats


def combine_kernel(got_ref, keep_ref, out_ref, lse_ref, stat):
    devices, height, tokens = got_ref.shape
    share = (height - 8) // 2
    for v in range(devices):
        rows = got_ref[v, 2 * share :, :].astype(F32)
        stat[0, v : v + 1, :] = rows[0:1, :] + rows[1:2, :] + rows[2:3, :]
        stat[1, v : v + 1, :] = rows[3:4, :] + rows[4:5, :]
        stat[2, v : v + 1, :] = rows[5:6, :] + rows[6:7, :] + rows[7:8, :]
    tops = stat[0]
    own = jnp.max(stat[2], axis=0, keepdims=True)
    top = jnp.maximum(jnp.max(tops, axis=0, keepdims=True), own)
    scale = jnp.exp(tops - top)
    rest = jnp.sum(scale * stat[1], axis=0, keepdims=True)
    total = rest + jnp.exp(own - top)
    lse_ref[...] = top + jnp.log(total)
    keep = keep_ref[...].astype(F32)
    stat[0] = scale * (keep / total)
    gone = keep * (rest / total)
    part = jnp.zeros((share, tokens), F32)
    hot = jnp.zeros((share, tokens), F32)
    for v in range(devices):
        part += stat[0, v : v + 1, :] * got_ref[v, 0:share, :].astype(F32)
        hot += got_ref[v, share : 2 * share, :].astype(F32)
    outer = (part - gone * hot).astype(BF16)
    out_ref[...] = outer


def grad_kernel(logit_ref, lse_ref, tgt_ref, keep_ref, pan_ref, out_ref, made, sems):
    cols = lax.broadcasted_iota(jnp.int32, logit_ref.shape, 0)
    hot = cols == tgt_ref[...] - lax.axis_index("voc") * logit_ref.shape[0]
    soft = jnp.exp(logit_ref[...] - lse_ref[...])
    keep = keep_ref[...].astype(F32)
    grad = ((soft - hot.astype(F32)) * keep).astype(BF16)
    blocks = sems.shape[0]
    rows = made.shape[0] // blocks
    copies = []
    for i in range(blocks):
        at = slice(rows * i, rows * (i + 1))
        made[at, :] = jnp.dot(pan_ref[at, :], grad, preferred_element_type=F32).astype(BF16)
        copies.append(pltpu.make_async_copy(made.at[at, :], out_ref.at[at, :], sems.at[i]))
        copies[-1].start()
    for copy in copies:
        copy.wait()


def pair_kernel(own_ref, near_ref, out_ref):
    out_ref[0] = own_ref[...]
    out_ref[1] = near_ref[...]


def assemble_kernel(pair_ref, far_ref, out_ref):
    mine = lax.axis_index("voc") // 8
    out_ref[mine] = pair_ref[0]
    out_ref[mine ^ 1] = pair_ref[1]
    out_ref[mine ^ 3] = far_ref[0]
    out_ref[mine ^ 2] = far_ref[1]


def total_kernel(parts_ref, out_ref):
    def add(k, total):
        return total + parts_ref[k].astype(F32)

    devices = parts_ref.shape[0]
    total = lax.fori_loop(1, devices, add, parts_ref[0].astype(F32), unroll=4)
    out_ref[...] = total.astype(BF16)


def scores_kernel(outer_ref, inner_ref, store_hbm, out_ref, query, wide, store_ref, sem, *sums):
    groups, rank, tokens = outer_ref.shape
    half = rank // 2
    low = lax.broadcasted_iota(jnp.int32, (8, 128), 1) < rank
    eight = lax.broadcasted_iota(jnp.int32, (8, tokens), 0).astype(F32)

    def multiply(k, even_ref, odd_ref):
        span = inner_ref[k, rank:, :].astype(F32)
        block = jnp.floor(span * 0.125)
        row = span - 8.0 * block
        mask = (row == eight).astype(F32)
        mask = jnp.concatenate([mask, mask], axis=0).astype(BF16)
        for c in (0, 1):
            wide[c] = inner_ref[k, 0:rank, 128 * c : 128 * (c + 1)].astype(F32)
        outer = outer_ref[k]
        shares = []
        for j in range(4):
            chosen = (block == float(j)).astype(F32)
            chosen = jnp.concatenate([chosen, chosen], axis=0).astype(BF16)
            shares.append(outer * jnp.concatenate([chosen] * (rank // 16), axis=0))
        for ref, side, order in ((even_ref, 0, (0, 1, 2, 3)), (odd_ref, 1, (1, 0, 3, 2))):
            columns = []
            for c in (0, 1):
                part = mask[:, 128 * c : 128 * (c + 1)]
                rows = [wide[c, pl.ds(2 * p + side, 8, stride=0), :] for p in range(half)]
                pairs = [jnp.concatenate(rows[p : p + 2], axis=0).astype(BF16) for p in range(0, half, 2)]
                columns.append(jnp.concatenate([x * part for x in pairs], axis=0))
            left = jnp.concatenate(columns, axis=1)
            right = jnp.concatenate([shares[j] for j in order], axis=0)
            ref[...] = lax.dot_general(left, right, LANES_BOTH, preferred_element_type=F32)

    def arrange(k, even_ref, odd_ref):
        base = pl.multiple_of(k * SPAN_DEV, SPAN_DEV)
        for pair in range(half):
            for c in (0, 1):
                x = even_ref[8 * pair : 8 * (pair + 1), 128 * c : 128 * (c + 1)]
                y = odd_ref[8 * pair : 8 * (pair + 1), 128 * c : 128 * (c + 1)]
                straight = jnp.where(low, x, y)
                crossed = pltpu.roll(jnp.where(low, y, x), rank, axis=1)
                query[pl.ds(base + 16 * c, 16), 128 * pair : 128 * (pair + 1)] = (
                    jnp.concatenate([straight, crossed], axis=0).astype(BF16)
                )

    first, second = sums[0:2], sums[2:4]
    fetch = pltpu.make_async_copy(store_hbm, store_ref, sem)
    fetch.start()

    def both(step, carry):
        for k in range(8):
            now, before = (first, second) if k % 2 == 0 else (second, first)
            multiply(8 * step + k, *now)
            arrange(lax.rem(8 * step + k + groups - 1, groups), *before)
        return carry

    lax.fori_loop(0, groups // 8, both, 0)
    arrange(groups - 1, *second)

    fetch.wait()
    result = lax.dot_general(query[...], store_ref[...], LANES_BOTH, preferred_element_type=F32)
    out_ref[...] = result * (1.0 / RANK)


def body(hidden, panel, in_proj, out_proj, targets, keep, span_ids, store):
    tokens, width = hidden.shape
    cols = panel.shape[1]
    devices = lax.axis_size("voc")
    share = width // devices
    steps = 4
    piece = width // steps
    classes = 4
    height = 2 * RANK // classes + 8
    inputs = (hidden, panel, in_proj.T, out_proj.T, targets[None], span_ids[None])
    logit, msg, inner = call(
        functools.partial(logits_kernel, classes),
        (
            jax.ShapeDtypeStruct((cols, tokens), F32),
            jax.ShapeDtypeStruct((devices, height, tokens), BF16),
            jax.ShapeDtypeStruct((RANK + 8, tokens), BF16),
        ),
        in_specs=[pl.BlockSpec(memory_space=pltpu.HBM)] * 6,
        out_specs=tuple(vmem(3)),
        scratch_shapes=[
            pltpu.VMEM((steps, tokens, piece), BF16),
            pltpu.VMEM((steps, piece, cols), BF16),
            pltpu.VMEM((RANK, width), BF16),
            pltpu.VMEM((RANK, cols), BF16),
            pltpu.VMEM((1, tokens), jnp.int32),
            pltpu.VMEM((1, tokens), jnp.int32),
            pltpu.VMEM((tokens, cols), F32),
            pltpu.VMEM((RANK, tokens), F32),
            pltpu.SemaphoreType.DMA((2 * steps + 4,)),
        ],
        name="logits",
    )(*(pltpu.with_memory_space_constraint(x, pltpu.HBM) for x in inputs))
    peers = devices // classes
    everyone = [[z + peers * x for z in range(peers) for x in range(classes)]]
    got = lax.all_to_all(msg, "voc", 0, 0, tiled=True, axis_index_groups=everyone)
    all_inner = lax.all_gather(inner, "tok", axis=0)
    got, all_inner = lax.optimization_barrier((got, all_inner))
    outer, lse = call(
        combine_kernel,
        (
            jax.ShapeDtypeStruct((RANK // classes, tokens), BF16),
            jax.ShapeDtypeStruct((1, tokens), F32),
        ),
        in_specs=vmem(2),
        out_specs=tuple(vmem(2)),
        scratch_shapes=[pltpu.VMEM((3, devices, tokens), F32)],
        name="combine",
    )(resident(got), keep[None])
    near = lax.ppermute(outer, "voc", [(v, v ^ 8) for v in range(devices)])
    partial = call(
        grad_kernel,
        jax.ShapeDtypeStruct((width, tokens), BF16),
        in_specs=vmem(5),
        out_specs=pl.BlockSpec(memory_space=pltpu.HBM),
        scratch_shapes=[
            pltpu.VMEM((width, tokens), BF16),
            pltpu.SemaphoreType.DMA((8,)),
        ],
        name="grad",
    )(resident(logit), resident(lse), targets[None], keep[None], resident(panel))
    partial = partial.reshape(devices, share, tokens)
    parts = lax.all_to_all(partial, "voc", 0, 0, tiled=True)
    pair = call(
        pair_kernel,
        jax.ShapeDtypeStruct((2, RANK // classes, tokens), BF16),
        in_specs=vmem(2),
        out_specs=vmem(1)[0],
        name="pair",
    )(resident(outer), resident(near))
    far = lax.ppermute(pair, "voc", [(v, v ^ 24) for v in range(devices)])
    outer = call(
        assemble_kernel,
        jax.ShapeDtypeStruct((classes, RANK // classes, tokens), BF16),
        in_specs=vmem(2),
        out_specs=vmem(1)[0],
        name="assemble",
    )(resident(pair), resident(far))
    all_outer = lax.all_gather(outer.reshape(RANK, tokens), "tok", axis=0)
    groups = all_outer.shape[0]
    scores = call(
        scores_kernel,
        jax.ShapeDtypeStruct((groups * SPAN_DEV, store.shape[0]), F32),
        in_specs=vmem(2) + [pl.BlockSpec(memory_space=pltpu.HBM)],
        out_specs=vmem(1)[0],
        scratch_shapes=[pltpu.VMEM((groups * SPAN_DEV, RANK * RANK), BF16)]
        + [pltpu.VMEM((2, RANK, 128), F32)]
        + [pltpu.VMEM(store.shape, BF16), pltpu.SemaphoreType.DMA]
        + [pltpu.VMEM((RANK * 4, RANK * 4), F32)] * 4,
        name="scores",
    )(resident(all_outer), resident(all_inner), pltpu.with_memory_space_constraint(store, pltpu.HBM))
    hidden_grad = call(
        total_kernel,
        jax.ShapeDtypeStruct((share, tokens), BF16),
        in_specs=vmem(1),
        out_specs=vmem(1)[0],
        name="total",
    )(resident(parts)).T
    return (hidden_grad, scores)


def solution(mesh):
    placed = (
        P("tok", None),
        P(None, "voc"),
        P(),
        P("voc", None),
        P("tok"),
        P("tok"),
        P("tok"),
        P(("tok", "voc"), None),
    )

    return jax.shard_map(
        body,
        mesh=mesh,
        in_specs=placed,
        out_specs=(P("tok", "voc"), P(None, ("tok", "voc"))),
        check_vma=False,
    )
```
